32 devices in a mesh: wide: 4 (over y, core), sixteen: 8 (over z, x).
Axes of the slice: x: 2, y: 2, z: 4, core: 2. Of those that a mesh axis runs over, the one named last changes fastest.
Arguments:
- observations: float32 [64, 256, 512], P(None, 'sixteen', 'wide'), may hold values from -60 to 60
- huber_scale: float32 [64], replicated, may hold values from 0.5 to 2
- observed: int32 [256, 512], P('sixteen', 'wide'), may hold values from 0 to 1, as said below
- jitter: float32 [2, 256, 512], P(None, 'sixteen', 'wide'), may hold values from -0.4 to 0.4
- owner_map: int32 [4, 64], P('wide'), may hold values from 0 to 7, as said below
- neighbours: int32 [4, 64, 6], P('wide'), may hold values from 0 to 63, as said below
Outputs:
- solution: float32 [4, 8, 64, 8, 512], P('wide', 'sixteen')
- residual: float32 [4, 8, 64, 8, 512], P('wide', 'sixteen')
The draws below stay inside these ranges and needn't reach their ends.
Inputs may be any that keep to these rules, and one draw needn't show every extreme that they name: At least one whole lattice row and at least one whole lattice column hold no observed point. `owner_map`: in each column group every device along sixteen holds 8 blocks (block g on device g // 8) and sends them to 8 different owners; every owner receives exactly 8 blocks, each from a different device. `neighbours`: block g of a column group lists g + d and g - d modulo 64 for each of half of 6 different offsets d between 1 and 4; all blocks of one group use the same offsets, so every list holds 6 different blocks and the relation is symmetric.
All inputs are finite; a program needn't handle non-finite values.
Results may differ from the reference program's by a relative error of at most 0.0003.
Values sent between devices are 32-bit elements; how exact they have to be, the bound alone decides.
A program may use at most 192 MiB of HBM per device.

```python
import math
import jax
import jax.numpy as jnp
from jax import lax

FIELDS = 64
BLOCK = 512
COL_DEV = 128
BLOCKS_DEV = 8
REACH = 4
NEIGHBOURS = 6
SWEEPS = 2
ITERS = 2
STRIP = 4
NSTRIPS = 64
NROW = 256
NCOL = 512
N_WIDE = 4
N_SIXTEEN = 8


def draw_observations(key, part):
    first_key, second_key, third_key, random_key_four = jax.random.split(jax.random.fold_in(key, 11), 4)
    lattice_dimensions = (FIELDS, NROW, NCOL)
    row_coefficients = jax.random.normal(first_key, (FIELDS, NROW, 1), jnp.float32)
    column_coefficients = jax.random.normal(second_key, (FIELDS, 1, NCOL), jnp.float32)
    gaussian_jitter = jax.random.normal(third_key, lattice_dimensions, jnp.float32)
    outlier_spikes = jnp.where(jax.random.uniform(random_key_four, lattice_dimensions, jnp.float32) < 0.05, 6.0, 0.0) * jnp.sign(gaussian_jitter + 0.001)
    observed_values = 1.5 * row_coefficients + 1.5 * column_coefficients + gaussian_jitter + outlier_spikes
    return jnp.clip(observed_values, -60.0, 60.0).astype(jnp.float32)


def draw_observed(key, part):
    first_key, second_key, third_key = jax.random.split(jax.random.fold_in(key, 53), 3)
    base = jax.random.randint(first_key, (NROW, NCOL), 0, 8) < 7
    empty_rows = jax.random.randint(second_key, (2,), 0, NROW)
    empty_cols = jax.random.randint(third_key, (2,), 0, NCOL)
    rows_hit = jnp.any(jnp.arange(NROW, dtype=jnp.int32)[:, None] == empty_rows[None, :], axis=1)
    cols_hit = jnp.any(jnp.arange(NCOL, dtype=jnp.int32)[:, None] == empty_cols[None, :], axis=1)
    cleared = rows_hit[:, None] | cols_hit[None, :]
    return jnp.where(cleared, 0, base.astype(jnp.int32)).astype(jnp.int32)


def draw_owner_map(key, part):

    def one_group(group_key):
        first_key, second_key, third_key = jax.random.split(group_key, 3)
        sources = jax.random.permutation(first_key, N_SIXTEEN)
        owners = jax.random.permutation(second_key, N_SIXTEEN)
        orders = jax.vmap(lambda order_key: jax.random.permutation(order_key, BLOCKS_DEV))(jax.random.split(third_key, N_SIXTEEN))
        return owners[(sources[:, None] + orders) % N_SIXTEEN].reshape(-1)
    group_keys = jax.random.split(jax.random.fold_in(key, 23), N_WIDE)
    return jax.vmap(one_group)(group_keys).astype(jnp.int32)


def draw_neighbours(key, part):
    total_strips = BLOCKS_DEV * N_SIXTEEN

    def one_group(group_key):
        offsets = jax.random.permutation(group_key, REACH)[:NEIGHBOURS // 2] + 1
        signed = jnp.stack([offsets, -offsets], axis=1).reshape(-1)
        numbers = jnp.arange(total_strips, dtype=jnp.int32)
        return (numbers[:, None] + signed[None, :]) % total_strips
    group_keys = jax.random.split(jax.random.fold_in(key, 37), N_WIDE)
    return jax.vmap(one_group)(group_keys).astype(jnp.int32)


def level_of(key, shape, cuts, least, top_value):
    def one(position, blocks):
        draws = jax.random.uniform(jax.random.fold_in(jax.random.fold_in(key, 6), position), (blocks,), jnp.float32, least / len(cuts), top_value / len(cuts))
        return jnp.repeat(jnp.exp(draws), shape[position] // blocks).reshape((-1,) + (1,) * (len(shape) - position - 1))

    level = one(*cuts[0])
    for cut in cuts[1:]:
        level = level * one(*cut)
    return level


def setup_inputs(seed: int = 0) -> dict:
    arg_keys = jax.random.split(jax.random.key(seed), 7)
    observations = draw_observations(jax.random.fold_in(arg_keys[6], 71), 0)
    huber_scale = jnp.clip(jnp.exp(jax.random.uniform(arg_keys[1], (FIELDS,), jnp.float32, math.log(0.5), math.log(2.0))), 0.5, 2.0)
    observed = draw_observed(jax.random.fold_in(arg_keys[6], 71), 0)
    jitter = jnp.clip(jax.random.uniform(arg_keys[3], (2, NROW, NCOL), jnp.float32, -0.4, 0.4) * level_of(arg_keys[3], (2, NROW, NCOL), ((1, 8), (2, 4)), -0.4, 0.0), -0.4, 0.4)
    owner_map = draw_owner_map(jax.random.fold_in(arg_keys[6], 71), 0)
    neighbours = draw_neighbours(jax.random.fold_in(arg_keys[6], 71), 0)
    return {"observations": observations, "huber_scale": huber_scale, "observed": observed, "jitter": jitter, "owner_map": owner_map, "neighbours": neighbours}


HUBER_EDGE = 1.345
NUGGET_TERM = 1.0
SILL_TERM = 0.02
ROOT_THREE = 1.7320508075688772
EXACT = lax.Precision.HIGHEST

def covariance(centre, others, strip_rows):
    spread = 2.0 * strip_rows
    cutoff = 6.0 * strip_rows
    row_gap = others[0][:, :, None] - centre[0][None, None, :]
    col_gap = others[1][:, :, None] - centre[1][None, None, :]
    distance = jnp.sqrt(row_gap * row_gap + col_gap * col_gap)
    scaled = ROOT_THREE * distance / spread
    fading = jnp.maximum(1.0 - distance / cutoff, 0.0)
    return SILL_TERM * (1.0 + scaled) * jnp.exp(-scaled) * fading ** 4 * (1.0 + 4.0 * distance / cutoff)

def owned_table(group_map, owners, per_owner):
    total_strips = group_map.shape[0]
    member = (group_map[None, :] == jnp.arange(owners, dtype=jnp.int32)[:, None]).astype(jnp.int32)
    ranked = jnp.cumsum(member, axis=1, dtype=jnp.int32) - 1
    slot_hit = (ranked[:, :, None] == jnp.arange(per_owner, dtype=jnp.int32)[None, None, :]).astype(jnp.int32) * member[:, :, None]
    numbers = jnp.arange(total_strips, dtype=jnp.int32)
    return lax.optimization_barrier(jnp.sum(slot_hit * numbers[None, :, None], axis=1, dtype=jnp.int32))

def apply_operator(direction, centres, neighbours):

    def one_block(flat_index):
        group = flat_index // NSTRIPS
        strip_number = flat_index % NSTRIPS
        group_values = direction[group]
        group_places = centres[group]
        listed = neighbours[group, strip_number]
        own = group_values[:, strip_number]
        near = jnp.take(group_values, listed, axis=1)
        centre = group_places[:, strip_number]
        others = jnp.concatenate([centre[:, None], jnp.take(group_places, listed, axis=1)], axis=1)
        kernel = covariance(centre, others, STRIP)
        stacked = jnp.concatenate([(NEIGHBOURS + 1.0) * own[:, None], near], axis=1)
        return NUGGET_TERM * own + jnp.einsum('fmb,mba->fa', stacked, kernel, precision=EXACT)
    result = lax.map(one_block, jnp.arange(N_WIDE * NSTRIPS, dtype=jnp.int32))
    return result.reshape(N_WIDE, NSTRIPS, FIELDS, BLOCK).transpose(0, 2, 1, 3)

def blocked(observed_values):
    depth = observed_values.shape[0]
    shaped = observed_values.reshape(depth, NSTRIPS, STRIP, N_WIDE, COL_DEV)
    return shaped.transpose(3, 0, 1, 2, 4).reshape(N_WIDE, depth, NSTRIPS, BLOCK)

def reference(observations, huber_scale, observed, jitter, owner_map, neighbours):
    weight = observed.astype(jnp.float32)
    row_count = jnp.maximum(lax.optimization_barrier(jnp.sum(weight, axis=1)), 1.0)
    col_count = jnp.maximum(lax.optimization_barrier(jnp.sum(weight, axis=0)), 1.0)
    spread_scale = huber_scale[:, None, None]
    row_effect = jnp.zeros((FIELDS, NROW), jnp.float32)
    col_effect = jnp.zeros((FIELDS, NCOL), jnp.float32)
    for sweep_number in range(SWEEPS):
        clipped = jnp.clip((observations - row_effect[:, :, None] - col_effect[:, None, :]) / spread_scale, -HUBER_EDGE, HUBER_EDGE)
        row_effect = row_effect + huber_scale[:, None] * lax.optimization_barrier(jnp.sum(weight[None] * clipped, axis=2)) / row_count[None, :]
        clipped = jnp.clip((observations - row_effect[:, :, None] - col_effect[:, None, :]) / spread_scale, -HUBER_EDGE, HUBER_EDGE)
        col_effect = col_effect + huber_scale[:, None] * lax.optimization_barrier(jnp.sum(weight[None] * clipped, axis=1)) / col_count[None, :]
    residual_field = weight[None] * (observations - row_effect[:, :, None] - col_effect[:, None, :])
    row_place = jnp.arange(NROW, dtype=jnp.int32).astype(jnp.float32)
    col_place = jnp.arange(NCOL, dtype=jnp.int32).astype(jnp.float32)
    location = jnp.stack([row_place[:, None] + jitter[0], col_place[None, :] + jitter[1]])
    right_side = blocked(residual_field)
    centres = blocked(location)
    solution_now = jnp.zeros_like(right_side)
    residual_now = right_side
    direction = right_side
    norm_now = lax.optimization_barrier(jnp.sum(residual_now * residual_now, axis=(0, 2, 3)))
    for number in range(ITERS):
        image = apply_operator(direction, centres, neighbours)
        alpha = norm_now / lax.optimization_barrier(jnp.sum(direction * image, axis=(0, 2, 3)))
        solution_now = solution_now + alpha[None, :, None, None] * direction
        residual_now = residual_now - alpha[None, :, None, None] * image
        if number + 1 < ITERS:
            norm_next = lax.optimization_barrier(jnp.sum(residual_now * residual_now, axis=(0, 2, 3)))
            direction = residual_now + (norm_next / norm_now)[None, :, None, None] * direction
            norm_now = norm_next
    table = jax.vmap(lambda group_map: owned_table(group_map, N_SIXTEEN, BLOCKS_DEV))(owner_map)

    def place(observed_values):

        def one_group(group_values, group_table):
            picked = jnp.take(group_values, group_table.reshape(-1), axis=1)
            return picked.reshape(FIELDS, N_SIXTEEN, BLOCKS_DEV, BLOCK).transpose(1, 0, 2, 3)
        return jax.vmap(one_group)(observed_values, table)
    return (place(solution_now), place(residual_now))
```

```python
import functools

import jax
import jax.numpy as jnp
from jax import lax
from jax.experimental import pallas as pl
from jax.experimental.pallas import tpu as pltpu
from jax.sharding import PartitionSpec as P

BLOCK = 512
BLOCKS_DEV = 8
REACH = 4
NEIGHBOURS = 6
SWEEPS = 2

HUBER_EDGE = 1.345
NUGGET_TERM = 1.0
SILL_TERM = 0.02
ROOT_THREE = 1.7320508075688772
LOG2E = 1.4426950408889634
GROUP = 16
MESH = pl.DeviceIdType.MESH
VMEM = pl.BlockSpec(memory_space=pltpu.VMEM)
SMEM = pl.BlockSpec(memory_space=pltpu.SMEM)
F32 = jnp.float32


def say_hello(sizes):
    barrier = pltpu.get_barrier_semaphore()
    for axis, n in sizes:
        me = lax.axis_index(axis)

        def say(k, carry, axis=axis, n=n, me=me):
            pl.semaphore_signal(
                barrier, inc=1, device_id={axis: lax.rem(me + k, n)}, device_id_type=MESH
            )
            return carry

        lax.fori_loop(1, n, say, 0)


def hear_hello(sizes):
    pl.semaphore_wait(pltpu.get_barrier_semaphore(), sum(n - 1 for _, n in sizes))


def remote(src, dst, send, recv, axis, n, shift):
    return pltpu.make_async_remote_copy(
        src_ref=src,
        dst_ref=dst,
        send_sem=send,
        recv_sem=recv,
        device_id={axis: lax.rem(lax.axis_index(axis) + shift, n)},
        device_id_type=MESH,
    )


def start(copies):
    for c in copies:
        c.start()


def wait(copies):
    for c in copies:
        c.wait()


def spread_copies(buffer, axis, n, send, recv):
    return [
        remote(buffer.at[0], buffer.at[k], send.at[k], recv.at[k], axis, n, k) for k in range(1, n)
    ]


def gathered_sum(buffer, axis, n):
    me = lax.axis_index(axis)
    total = None
    for owner in range(n):
        term = buffer[lax.rem(me - owner + n, n)]
        total = term if total is None else total + term
    return total


def exchange_copies(staged, received, n, send, recv):
    return [pltpu.make_async_copy(staged.at[0], received.at[0], send.at[0])] + [
        remote(staged.at[k], received.at[k], send.at[k], recv.at[k], "sixteen", n, k)
        for k in range(1, n)
    ]


def edge_copies(source, target, reach, n, send, recv):
    rows = source.shape[0]
    return [
        remote(
            source.at[pl.ds(first, reach)],
            target.at[pl.ds(side * reach, reach)],
            send.at[side],
            recv.at[side],
            "sixteen",
            n,
            shift,
        )
        for side, first, shift in ((0, rows - reach, 1), (1, 0, n - 1))
    ]


def swap(x):
    return pltpu.roll(x, x.shape[-1] // 2, x.ndim - 1)


def fold(x):
    return x + swap(x)


def low_lanes(x):
    return lax.broadcasted_iota(jnp.int32, x.shape, x.ndim - 1) < x.shape[-1] // 2


def beside(even, odd):
    return jnp.where(low_lanes(even), even, odd)


def turned(x, size):
    rows = x.shape[0]
    if rows < size:
        x = jnp.concatenate([x, jnp.zeros((size - rows, x.shape[1]), x.dtype)], axis=0)
    return x.T


def across(x, k, shape):
    return jnp.broadcast_to(x[:, k : k + 1], shape)


def solve_kernel(
    nw, ns, fields, strip_rows, starts, span, static_came,
    owner, listed, came, obs_in, scale_in, seen_in, jitter_in,
    out, rest,
    offs, chosen,
    obs, weight, edge, q, q_edge, staged_p, recv_p, staged_q, recv_q, staged_w, recv_w,
    tiles, win, cb, oth, place, coords,
    scale, row_eff, row_cnt, col_eff, col_cnt, row_edge, row_buf0, row_buf1, col_buf0, col_buf1,
    dots, dot_w, dot_s,
    sem_s, sem_r, exch_s, exch_r, halo_s, halo_r,
):
    rows, cols, lanes = obs.shape
    half = cols // 2
    pairs = strip_rows // 2
    reach = REACH * pairs
    row_dev = 2 * rows
    row_reach = 2 * reach
    groups = len(starts)
    wide = strip_rows * span
    tile_rows = strip_rows * GROUP
    total_strips = BLOCKS_DEV * ns
    me = lax.axis_index("sixteen")
    group_me = lax.axis_index("wide")
    everyone = (("wide", nw), ("sixteen", ns))
    full = (cols, lanes)

    say_hello(everyone)

    def pack(r, carry):
        both = jnp.concatenate(
            [obs_in[pl.ds(2 * r + parity, fields, stride=row_dev), :] for parity in range(2)],
            axis=0,
        )
        obs[r] = both.T
        return carry

    lax.fori_loop(0, rows, pack, 0)

    row_number = lax.broadcasted_iota(jnp.int32, (row_dev, cols), 0) + me * row_dev
    col_number = lax.broadcasted_iota(jnp.int32, (row_dev, cols), 1) + group_me * cols
    seen = seen_in[...].astype(F32)
    place[0, pl.ds(row_reach, row_dev)] = row_number.astype(F32) + jitter_in[0]
    place[1, pl.ds(row_reach, row_dev)] = col_number.astype(F32) + jitter_in[1]
    place[2, pl.ds(row_reach, row_dev)] = seen

    for n in range(NEIGHBOURS):
        other = listed[n, 0]
        offs[n + 1] = jnp.where(other < total_strips // 2, other, other - total_strips)
    offs[0] = 0
    for k in range(ns):
        target = lax.rem(me + k, ns)
        pick = 0
        for j in range(BLOCKS_DEV):
            pick = jnp.where(owner[0, me * BLOCKS_DEV + j] == target, j, pick)
        chosen[k] = pick

    hear_hello(everyone)
    place_copies = [
        remote(
            place.at[:, pl.ds(row_dev, row_reach)],
            place.at[:, pl.ds(0, row_reach)],
            sem_s.at[6, 0], sem_r.at[6, 0], "sixteen", ns, 1,
        ),
        remote(
            place.at[:, pl.ds(row_reach, row_reach)],
            place.at[:, pl.ds(row_reach + row_dev, row_reach)],
            sem_s.at[6, 1], sem_r.at[6, 1], "sixteen", ns, ns - 1,
        ),
    ]
    obs_copies = edge_copies(obs, edge, reach, ns, sem_s.at[7], sem_r.at[7])
    row_copies = edge_copies(row_eff, row_edge, reach, ns, sem_s.at[8], sem_r.at[8])
    start(place_copies)
    start(obs_copies)

    seen_t = turned(seen, lanes)
    for r in range(rows):
        weight[r] = beside(across(seen_t, 2 * r, full), across(seen_t, 2 * r + 1, full))
    one_scale = scale_in[...]
    scale[...] = jnp.concatenate([one_scale, one_scale], axis=1)
    inv = 1.0 / scale[...]
    row_eff[...] = jnp.zeros_like(row_eff)
    col_eff[...] = jnp.zeros_like(col_eff)

    spread = 2.0 * strip_rows
    cutoff = 6.0 * strip_rows
    ratio = ROOT_THREE * cutoff / spread
    unit = (4.0 * ratio * SILL_TERM) ** (1.0 / 6.0)

    def prepare_places():
        coords[0] = (place[0] - (me * row_dev + row_dev // 2).astype(F32)) * (unit / cutoff)
        coords[1] = (place[1] - (group_me * cols + cols // 2).astype(F32)) * (unit / cutoff)
        for c in range(2):
            t = turned(coords[c, pl.ds(row_reach, row_dev)], lanes)
            for r in range(row_dev):
                cb[c, r] = across(t, r, full)
        for c in range(2):
            for pair in range(pairs):
                a = [
                    coords[c, pl.ds(2 * pair + parity, oth.shape[2], stride=strip_rows), :]
                    for parity in range(2)
                ]
                for i, s in enumerate(starts):
                    x = pltpu.roll(a[0], (cols - s) % cols, 1)
                    y = pltpu.roll(a[1], (cols + span - s) % cols, 1)
                    oth[i, c, :, pair * lanes : (pair + 1) * lanes] = beside(x, y)

    def build_tile(t, carry):
        block, i = t // groups, lax.rem(t, groups)
        at = pl.multiple_of(i * GROUP, GROUP)
        first = pl.multiple_of(block * strip_rows, strip_rows)
        row_here = cb[0, pl.ds(first, strip_rows), pl.ds(at, GROUP), :].reshape(tile_rows, lanes)
        col_here = cb[1, pl.ds(first, strip_rows), pl.ds(at, GROUP), :].reshape(tile_rows, lanes)
        for n in range(NEIGHBOURS + 1):
            h = block + REACH + offs[n]
            row_line = oth[i, 0, pl.ds(h, 1), :]
            col_line = oth[i, 1, pl.ds(h, 1), :]
            for part in range(wide // lanes):
                cut = slice(part * lanes, (part + 1) * lanes)
                row_gap = row_line[:, cut] - row_here
                col_gap = col_line[:, cut] - col_here
                square = row_gap * row_gap + col_gap * col_gap
                if n == 0:
                    distance = square * lax.rsqrt(jnp.maximum(square, 1e-30))
                else:
                    distance = square * lax.rsqrt(square)
                fading = jnp.maximum(unit - distance, 0.0)
                fading = fading * fading
                fading = fading * fading
                decay = jnp.exp2(distance * (-ratio * LOG2E / unit))
                lead = (distance + unit / ratio) * (distance + unit / 4.0)
                kernel = (lead * decay) * fading
                if n == 0:
                    kernel = kernel * (NEIGHBOURS + 1.0)
                high = kernel.astype(jnp.bfloat16)
                low = (kernel - high.astype(F32)).astype(jnp.bfloat16)
                base = n * wide + part * lanes
                tiles[block, i, 0:tile_rows, base : base + lanes] = high
                tiles[block, i, tile_rows : 2 * tile_rows, base : base + lanes] = low
        return carry

    steps = BLOCKS_DEV * groups
    quarter = steps // (2 * SWEEPS)

    def build_some(part):
        lax.fori_loop(part * quarter, (part + 1) * quarter, build_tile, 0)

    edge_value = HUBER_EDGE
    for sweep in range(SWEEPS):
        row_buf = (row_buf0, row_buf1)[min(sweep, 1)]
        col_buf = (col_buf0, col_buf1)[min(sweep, 1)]

        def clipped(r):
            value = (obs[r] - row_eff[pl.ds(r, 1)] - col_eff[...]) * inv
            return weight[r] * jnp.clip(value, -edge_value, edge_value)

        def row_step(r, carry):
            row_buf[0, pl.ds(r, 1)] = jnp.sum(clipped(r), axis=0, keepdims=True)
            if sweep == 0:
                row_buf[0, pl.ds(rows + r, 1)] = jnp.sum(weight[r], axis=0, keepdims=True)
            return carry

        lax.fori_loop(0, rows, row_step, 0)
        sums = spread_copies(row_buf, "wide", nw, sem_s.at[sweep], sem_r.at[sweep])
        start(sums)
        if sweep == 0:
            wait(place_copies)
            prepare_places()
        build_some(2 * sweep)
        wait(sums)
        total = gathered_sum(row_buf, "wide", nw)
        if sweep == 0:
            row_cnt[...] = jnp.maximum(total[rows:], 1.0)
        row_eff[...] = row_eff[...] + scale[...] * total[:rows] / row_cnt[...]
        if sweep == SWEEPS - 1:
            start(row_copies)

        def col_step(r, carry):
            return carry + clipped(r)

        part = fold(lax.fori_loop(0, rows, col_step, jnp.zeros(full, F32)))
        col_buf[0, pl.ds(0, half)] = beside(part[:half], part[half:])
        if sweep == 0:
            count = jnp.sum(seen, axis=0, keepdims=True)
            col_buf[0, pl.ds(half, 8)] = jnp.broadcast_to(count, (8, cols))
        sums = spread_copies(col_buf, "sixteen", ns, sem_s.at[2 + sweep], sem_r.at[2 + sweep])
        start(sums)
        build_some(2 * sweep + 1)
        wait(sums)
        total = gathered_sum(col_buf, "sixteen", ns)
        if sweep == 0:
            count = jnp.broadcast_to(total[half : half + 1], full).T
            col_cnt[...] = jnp.maximum(count, 1.0)
        y = total[:half]
        z = swap(y)
        both = jnp.concatenate([beside(y, z), beside(z, y)], axis=0)
        col_eff[...] = col_eff[...] + scale[...] * both / col_cnt[...]

    wait(obs_copies)

    def remain(r, carry):
        obs[r] = weight[r] * (obs[r] - row_eff[pl.ds(r, 1)] - col_eff[...])
        return carry

    lax.fori_loop(0, rows, remain, 0)
    p = obs

    def stage(staged, source):
        def one(k, carry):
            for pair in range(pairs):
                staged[k, pair] = source[chosen[k] * pairs + pair]
            return carry

        lax.fori_loop(0, ns, one, 0)

    stage(staged_p, p)
    p_copies = exchange_copies(staged_p, recv_p, ns, exch_s.at[0], exch_r.at[0])
    start(p_copies)

    def windows(source, first, h):
        for pair in range(pairs):
            x = source[first + pair]
            z = swap(x)
            low = low_lanes(x)
            for parity in range(2):
                y = jnp.where(low, x, z) if parity == 0 else jnp.where(low, z, x)
                high = y.astype(jnp.bfloat16).astype(F32)
                both = jnp.where(low, high, y - high)
                win[0, h, 2 * pair + parity] = both.astype(jnp.bfloat16)
                win[1, h, 2 * pair + parity, 0 : cols - GROUP] = both[
                    GROUP // 2 : cols - GROUP // 2
                ].astype(jnp.bfloat16)

    def own_windows(source):
        def one(b, carry):
            windows(source, b * pairs, REACH + b)
            return carry

        lax.fori_loop(0, BLOCKS_DEV, one, 0)

    def edge_windows(source):
        def one(b, carry):
            windows(source, b * pairs, b)
            windows(source, reach + b * pairs, REACH + BLOCKS_DEV + b)
            return carry

        lax.fori_loop(0, REACH, one, 0)

    own_windows(p)
    wait(row_copies)
    seen_t = turned(place[2], lanes)
    for t in range(reach):
        for at, r in ((t, t), (reach + t, reach + rows + t)):
            there = beside(across(seen_t, 2 * r, full), across(seen_t, 2 * r + 1, full))
            edge[at] = there * (edge[at] - row_edge[pl.ds(at, 1)] - col_eff[...])
    edge_windows(edge)
    dots[...] = jnp.zeros_like(dots)

    def apply(block, own_of, store):
        for i, s in enumerate(starts):
            shifted = (s % GROUP) // (GROUP // 2)
            base = s - shifted * (GROUP // 2)
            acc = jnp.zeros((2 * tile_rows, lanes), F32)
            for n in range(NEIGHBOURS + 1):
                h = block + REACH + offs[n]
                acc = acc + jnp.dot(
                    tiles[block, i, :, n * wide : (n + 1) * wide],
                    win[shifted, h, :, base : base + span, :].reshape(wide, lanes),
                    preferred_element_type=F32,
                )
            y = fold(acc[:tile_rows] + acc[tile_rows:])
            for pair in range(pairs):
                even = y[(2 * pair) * GROUP : (2 * pair + 1) * GROUP]
                odd = y[(2 * pair + 1) * GROUP : (2 * pair + 2) * GROUP]
                own = own_of(pair, i * GROUP)
                store(pair, i * GROUP, own, NUGGET_TERM * own + beside(even, odd))

    def gather_dot(k, x, y):
        z = x * y
        dots[k] = dots[k] + (z[: GROUP // 2] + z[GROUP // 2 :])

    def q_copies(t):
        return [
            remote(
                q.at[pl.ds((REACH + t) * pairs, pairs)],
                q_edge.at[pl.ds(t * pairs, pairs)],
                halo_s.at[0, t], halo_r.at[0, t], "sixteen", ns, 1,
            ),
            remote(
                q.at[pl.ds(t * pairs, pairs)],
                q_edge.at[pl.ds(reach + t * pairs, pairs)],
                halo_s.at[1, t], halo_r.at[1, t], "sixteen", ns, ns - 1,
            ),
        ]

    def first_block(block):
        def own_of(pair, at):
            return p[block * pairs + pair, at : at + GROUP, :]

        def store(pair, at, own, value):
            q[block * pairs + pair, at : at + GROUP, :] = value
            gather_dot(0, own, own)
            gather_dot(1, own, value)
            gather_dot(2, value, value)

        apply(block, own_of, store)

    def first_pass(t, carry):
        def one(side, inner):
            first_block(side * REACH + t)
            return inner

        lax.fori_loop(0, 2, one, 0)
        start(q_copies(t))
        return carry

    lax.fori_loop(0, REACH, first_pass, 0)

    stage(staged_q, q)
    q_exchange = exchange_copies(staged_q, recv_q, ns, exch_s.at[1], exch_r.at[1])
    start(q_exchange)
    own_windows(q)
    for t in range(REACH):
        wait(q_copies(t))
    edge_windows(q_edge)

    w_copies = exchange_copies(staged_w, recv_w, ns, exch_s.at[2], exch_r.at[2])
    one_each = ns == BLOCKS_DEV

    def second_block(g, carry):
        slot = lax.rem(g + 1, BLOCKS_DEV)
        block = chosen[slot] if one_each else g

        def own_of(pair, at):
            return q[block * pairs + pair, at : at + GROUP, :]

        def store(pair, at, own, value):
            gather_dot(3, own, value)
            if one_each:
                staged_w[slot, pair, at : at + GROUP, :] = value
            else:
                edge[g * pairs + pair, at : at + GROUP, :] = value

        apply(block, own_of, store)
        if one_each:
            for k in range(ns):

                @pl.when(g == (k - 1) % ns)
                def _(k=k):
                    w_copies[k].start()

        return carry

    lax.fori_loop(0, BLOCKS_DEV, second_block, 0)
    if not one_each:
        stage(staged_w, edge)
        start(w_copies)

    for k in range(4):
        dot_w[0, k : k + 1] = jnp.sum(fold(dots[k]), axis=0, keepdims=True)
    dot_w[0, 4:8] = jnp.zeros((4, lanes), F32)
    sums = spread_copies(dot_w, "wide", nw, sem_s.at[4], sem_r.at[4])
    start(sums)
    wait(sums)
    dot_s[0] = gathered_sum(dot_w, "wide", nw)
    sums = spread_copies(dot_s, "sixteen", ns, sem_s.at[5], sem_r.at[5])
    start(sums)
    wait(sums)
    total = gathered_sum(dot_s, "sixteen", ns)
    m0, m1, m2, m3 = (total[k : k + 1] for k in range(4))
    alpha = m0 / m1
    norm = (m0 - 2.0 * alpha * m1) + alpha * alpha * m2
    grown = 1.0 + norm / m0
    bend = grown * (grown * m1 - 2.0 * alpha * m2) + alpha * alpha * m3
    second = norm / bend
    near = alpha + second * grown
    far = second * alpha

    def slot_of(j):
        return lax.rem(me - j + ns, ns) if static_came else came[j]

    def put(target, j, pair, value):
        value = value.T
        for parity in range(2):
            at = (2 * pair + parity) * cols
            target[:, j, at : at + cols] = value[parity * fields : (parity + 1) * fields]

    wait(p_copies)
    wait(q_exchange)
    for j in range(BLOCKS_DEV):
        k = slot_of(j)
        for pair in range(pairs):
            put(out, j, pair, near * recv_p[k, pair] - far * recv_q[k, pair])
    wait(w_copies)
    for j in range(BLOCKS_DEV):
        k = slot_of(j)
        for pair in range(pairs):
            put(
                rest, j, pair,
                (recv_p[k, pair] - near * recv_q[k, pair]) + far * recv_w[k, pair],
            )


def owned_table(group_map, owners, per_owner):
    total_strips = group_map.shape[0]
    member = (group_map[None, :] == jnp.arange(owners, dtype=jnp.int32)[:, None]).astype(jnp.int32)
    ranked = jnp.cumsum(member, axis=1, dtype=jnp.int32) - 1
    slot_hit = (ranked[:, :, None] == jnp.arange(per_owner, dtype=jnp.int32)[None, None, :]).astype(
        jnp.int32
    ) * member[:, :, None]
    numbers = jnp.arange(total_strips, dtype=jnp.int32)
    return jnp.sum(slot_hit * numbers[None, :, None], axis=1, dtype=jnp.int32)


def on_device(observations, huber_scale, observed, jitter, owner_map, neighbours):
    fields, row_dev, col_dev = observations.shape
    nw, ns = lax.axis_size("wide"), lax.axis_size("sixteen")
    strip_rows = BLOCK // col_dev
    rows, lanes = row_dev // 2, 2 * fields
    pairs = strip_rows // 2
    reach = REACH * pairs
    shape = jax.ShapeDtypeStruct

    cut = 6 * strip_rows
    span = GROUP + 2 * cut
    starts = tuple(
        min(max(GROUP * i - cut, 0), col_dev - span) for i in range(col_dev // GROUP)
    )
    groups = len(starts)
    wide = strip_rows * span
    blocks_halo = BLOCKS_DEV + 2 * REACH

    static_came = ns == BLOCKS_DEV
    if static_came:
        came = jnp.zeros((BLOCKS_DEV,), jnp.int32)
    else:
        my_place = lax.axis_index("sixteen")
        table = owned_table(owner_map[0], ns, BLOCKS_DEV)
        my_ids = lax.dynamic_index_in_dim(table, my_place, 0, keepdims=False)
        came = (my_place - my_ids // BLOCKS_DEV + ns) % ns

    most = max(nw, ns)
    vm = lambda *s: pltpu.VMEM(s, F32)
    moved = (ns, pairs, col_dev, lanes)
    field = (rows, col_dev, lanes)
    place_rows = row_dev + 4 * reach
    out_shape = shape((fields, BLOCKS_DEV, BLOCK), F32)
    solution_now, residual_now = pl.pallas_call(
        functools.partial(solve_kernel, nw, ns, fields, strip_rows, starts, span, static_came),
        out_shape=(out_shape, out_shape),
        in_specs=[SMEM] * 3 + [VMEM] * 4,
        out_specs=(VMEM, VMEM),
        scratch_shapes=[
            pltpu.SMEM((NEIGHBOURS + 1,), jnp.int32),
            pltpu.SMEM((ns,), jnp.int32),
            vm(*field), vm(*field), vm(2 * reach, col_dev, lanes), vm(*field),
            vm(2 * reach, col_dev, lanes),
            vm(*moved), vm(*moved), vm(*moved), vm(*moved), vm(*moved), vm(*moved),
            pltpu.VMEM((BLOCKS_DEV, groups, 2 * strip_rows * GROUP, (NEIGHBOURS + 1) * wide), jnp.bfloat16),
            pltpu.VMEM((2, blocks_halo, strip_rows, col_dev, lanes), jnp.bfloat16),
            vm(2, row_dev, col_dev, lanes),
            vm(groups, 2, blocks_halo, wide),
            vm(3, place_rows, col_dev),
            vm(2, place_rows, col_dev),
            vm(1, lanes),
            vm(rows, lanes), vm(rows, lanes), vm(col_dev, lanes), vm(col_dev, lanes),
            vm(2 * reach, lanes),
            vm(nw, 2 * rows, lanes), vm(nw, rows, lanes),
            vm(ns, col_dev // 2 + 8, lanes), vm(ns, col_dev // 2, lanes),
            vm(4, 8, lanes), vm(nw, 8, lanes), vm(ns, 8, lanes),
            pltpu.SemaphoreType.DMA((9, most)), pltpu.SemaphoreType.DMA((9, most)),
            pltpu.SemaphoreType.DMA((3, ns)), pltpu.SemaphoreType.DMA((3, ns)),
            pltpu.SemaphoreType.DMA((2, REACH)), pltpu.SemaphoreType.DMA((2, REACH)),
        ],
        compiler_params=pltpu.CompilerParams(
            collective_id=0, has_side_effects=True, vmem_limit_bytes=66 * 1000 * 1000
        ),
    )(
        owner_map,
        neighbours[0].T,
        came,
        observations.reshape(fields * row_dev, col_dev),
        huber_scale.reshape(1, fields),
        observed,
        jitter,
    )
    return solution_now[None, None], residual_now[None, None]


def solution(mesh):
    return jax.shard_map(
        on_device,
        mesh=mesh,
        in_specs=(
            P(None, "sixteen", "wide"),
            P(),
            P("sixteen", "wide"),
            P(None, "sixteen", "wide"),
            P("wide", None),
            P("wide", None, None),
        ),
        out_specs=(P("wide", "sixteen", None, None, None), P("wide", "sixteen", None, None, None)),
        check_vma=False,
    )
```

```python
import functools

import jax
import jax.numpy as jnp
from jax import lax
from jax.experimental import pallas as pl
from jax.experimental.pallas import tpu as pltpu
from jax.sharding import PartitionSpec as P

BLOCK = 512
BLOCKS_DEV = 8
REACH = 4
NEIGHBOURS = 6
SWEEPS = 2

HUBER_EDGE = 1.345
NUGGET_TERM = 1.0
SILL_TERM = 0.02
ROOT_THREE = 1.7320508075688772
LOG2E = 1.4426950408889634
GROUP = 16
MESH = pl.DeviceIdType.MESH
VMEM = pl.BlockSpec(memory_space=pltpu.VMEM)
SMEM = pl.BlockSpec(memory_space=pltpu.SMEM)
F32 = jnp.float32


def say_hello(sizes):
    barrier = pltpu.get_barrier_semaphore()
    for axis, n in sizes:
        me = lax.axis_index(axis)

        def say(k, carry, axis=axis, n=n, me=me):
            pl.semaphore_signal(
                barrier, inc=1, device_id={axis: lax.rem(me + k, n)}, device_id_type=MESH
            )
            return carry

        lax.fori_loop(1, n, say, 0)


def hear_hello(sizes):
    pl.semaphore_wait(pltpu.get_barrier_semaphore(), sum(n - 1 for _, n in sizes))


def remote(src, dst, send, recv, axis, n, shift):
    return pltpu.make_async_remote_copy(
        src_ref=src,
        dst_ref=dst,
        send_sem=send,
        recv_sem=recv,
        device_id={axis: lax.rem(lax.axis_index(axis) + shift, n)},
        device_id_type=MESH,
    )


def start(copies):
    for c in copies:
        c.start()


def wait(copies):
    for c in copies:
        c.wait()


def spread_copies(buffer, axis, n, send, recv):
    return [
        remote(buffer.at[0], buffer.at[k], send.at[k], recv.at[k], axis, n, k) for k in range(1, n)
    ]


def gathered_sum(buffer, axis, n):
    me = lax.axis_index(axis)
    total = None
    for owner in range(n):
        term = buffer[lax.rem(me - owner + n, n)]
        total = term if total is None else total + term
    return total


def exchange_copies(staged, received, n, send, recv):
    return [pltpu.make_async_copy(staged.at[0], received.at[0], send.at[0])] + [
        remote(staged.at[k], received.at[k], send.at[k], recv.at[k], "sixteen", n, k)
        for k in range(1, n)
    ]


def edge_copies(source, target, reach, n, send, recv):
    rows = source.shape[0]
    return [
        remote(
            source.at[pl.ds(first, reach)],
            target.at[pl.ds(side * reach, reach)],
            send.at[side],
            recv.at[side],
            "sixteen",
            n,
            shift,
        )
        for side, first, shift in ((0, rows - reach, 1), (1, 0, n - 1))
    ]


def swap(x):
    return pltpu.roll(x, x.shape[-1] // 2, x.ndim - 1)


def fold(x):
    return x + swap(x)


def low_lanes(x):
    return lax.broadcasted_iota(jnp.int32, x.shape, x.ndim - 1) < x.shape[-1] // 2


def beside(even, odd):
    return jnp.where(low_lanes(even), even, odd)


def turned(x, size):
    rows = x.shape[0]
    if rows < size:
        x = jnp.concatenate([x, jnp.zeros((size - rows, x.shape[1]), x.dtype)], axis=0)
    return x.T


def across(x, k, shape):
    return jnp.broadcast_to(x[:, k : k + 1], shape)


def solve_kernel(
    nw, ns, fields, strip_rows, starts, span, static_came,
    owner, listed, came, obs_in, scale_in, seen_in, jitter_in,
    out, rest,
    offs, chosen,
    obs, weight, edge, q, q_edge, staged_p, recv_p, staged_q, recv_q, staged_w, recv_w,
    staged_m, recv_m, tiles, win, cb, oth, place, coords,
    scale, row_eff, row_cnt, col_eff, col_cnt, row_edge, row_buf0, row_buf1,
    col_part, col_send0, col_send1, col_got0, col_got1, col_all0, col_all1,
    dots, dot_w, dot_s,
    sem_s, sem_r, exch_s, exch_r, obs_s, obs_r, halo_s, halo_r,
):
    rows, cols, lanes = obs.shape
    half = cols // 2
    chunk = half // ns
    pairs = strip_rows // 2
    reach = REACH * pairs
    row_dev = 2 * rows
    row_reach = 2 * reach
    groups = len(starts)
    wide = strip_rows * span
    tile_rows = strip_rows * GROUP
    total_strips = BLOCKS_DEV * ns
    me = lax.axis_index("sixteen")
    group_me = lax.axis_index("wide")
    everyone = (("wide", nw), ("sixteen", ns))
    full = (cols, lanes)

    say_hello(everyone)

    def pack(r, carry):
        both = jnp.concatenate(
            [obs_in[pl.ds(2 * r + parity, fields, stride=row_dev), :] for parity in range(2)],
            axis=0,
        )
        obs[r] = both.T
        return carry

    lax.fori_loop(0, rows, pack, 0)

    row_number = lax.broadcasted_iota(jnp.int32, (row_dev, cols), 0) + me * row_dev
    col_number = lax.broadcasted_iota(jnp.int32, (row_dev, cols), 1) + group_me * cols
    seen = seen_in[...].astype(F32)
    place[0, pl.ds(row_reach, row_dev)] = row_number.astype(F32) + jitter_in[0]
    place[1, pl.ds(row_reach, row_dev)] = col_number.astype(F32) + jitter_in[1]
    place[2, pl.ds(row_reach, row_dev)] = seen

    for n in range(NEIGHBOURS):
        other = listed[n, 0, 0]
        offs[n + 1] = jnp.where(other < total_strips // 2, other, other - total_strips)
    offs[0] = 0
    for k in range(ns):
        target = lax.rem(me + k, ns)
        pick = 0
        for j in range(BLOCKS_DEV):
            pick = jnp.where(owner[0, me * BLOCKS_DEV + j] == target, j, pick)
        chosen[k] = pick

    hear_hello(everyone)
    place_copies = [
        remote(
            place.at[:, pl.ds(row_dev, row_reach)],
            place.at[:, pl.ds(0, row_reach)],
            sem_s.at[6, 0], sem_r.at[6, 0], "sixteen", ns, 1,
        ),
        remote(
            place.at[:, pl.ds(row_reach, row_reach)],
            place.at[:, pl.ds(row_reach + row_dev, row_reach)],
            sem_s.at[6, 1], sem_r.at[6, 1], "sixteen", ns, ns - 1,
        ),
    ]

    def halo_copies(source, target, size, send, recv, t):
        return [
            remote(
                source.at[pl.ds(rows - reach + t * size, size)],
                target.at[pl.ds(t * size, size)],
                send.at[0, t], recv.at[0, t], "sixteen", ns, 1,
            ),
            remote(
                source.at[pl.ds(t * size, size)],
                target.at[pl.ds(reach + t * size, size)],
                send.at[1, t], recv.at[1, t], "sixteen", ns, ns - 1,
            ),
        ]

    obs_copies = [halo_copies(obs, edge, 1, obs_s, obs_r, t) for t in range(reach)]
    row_copies = edge_copies(row_eff, row_edge, reach, ns, sem_s.at[8], sem_r.at[8])
    start(place_copies)

    def stage(staged, source):
        def one(k, carry):
            for pair in range(pairs):
                staged[k, pair] = source[chosen[k] * pairs + pair]
            return carry

        lax.fori_loop(0, ns, one, 0)

    stage(staged_p, obs)
    p_copies = exchange_copies(staged_p, recv_p, ns, exch_s.at[0], exch_r.at[0])

    near_first = p_copies[2::2]
    bulk = [
        p_copies[:1] + sum(obs_copies[0:3], []) + near_first[0::3],
        sum(obs_copies[3:4], []),
        sum(obs_copies[4:6], []) + near_first[1::3],
        sum(obs_copies[6:7], []),
        sum(obs_copies[7:8], []) + near_first[2::3] + p_copies[1::2],
    ]
    start(bulk[0])
    seen_t = turned(seen, lanes)
    for r in range(rows):
        weight[r] = beside(across(seen_t, 2 * r, full), across(seen_t, 2 * r + 1, full))
    one_scale = scale_in[...]
    scale[...] = jnp.concatenate([one_scale, one_scale], axis=1)
    inv = 1.0 / scale[...]
    row_eff[...] = jnp.zeros_like(row_eff)
    col_eff[...] = jnp.zeros_like(col_eff)

    spread = 2.0 * strip_rows
    cutoff = 6.0 * strip_rows
    ratio = ROOT_THREE * cutoff / spread
    unit = (4.0 * ratio * SILL_TERM) ** (1.0 / 6.0)

    def prepare_places():
        coords[0] = (place[0] - (me * row_dev + row_dev // 2).astype(F32)) * (unit / cutoff)
        coords[1] = (place[1] - (group_me * cols + cols // 2).astype(F32)) * (unit / cutoff)
        for c in range(2):
            t = turned(coords[c, pl.ds(row_reach, row_dev)], lanes)
            for r in range(row_dev):
                cb[c, r] = across(t, r, full)
        for c in range(2):
            for pair in range(pairs):
                a = [
                    coords[c, pl.ds(2 * pair + parity, oth.shape[2], stride=strip_rows), :]
                    for parity in range(2)
                ]
                for i, s in enumerate(starts):
                    x = pltpu.roll(a[0], (cols - s) % cols, 1)
                    y = pltpu.roll(a[1], (cols + span - s) % cols, 1)
                    oth[i, c, :, pair * lanes : (pair + 1) * lanes] = beside(x, y)

    def build_tile(t, carry):
        block, i = t // groups, lax.rem(t, groups)
        at = pl.multiple_of(i * GROUP, GROUP)
        first = pl.multiple_of(block * strip_rows, strip_rows)
        row_here = cb[0, pl.ds(first, strip_rows), pl.ds(at, GROUP), :].reshape(tile_rows, lanes)
        col_here = cb[1, pl.ds(first, strip_rows), pl.ds(at, GROUP), :].reshape(tile_rows, lanes)
        for n in range(NEIGHBOURS + 1):
            h = block + REACH + offs[n]
            row_line = oth[i, 0, pl.ds(h, 1), :]
            col_line = oth[i, 1, pl.ds(h, 1), :]
            for part in range(wide // lanes):
                cut = slice(part * lanes, (part + 1) * lanes)
                row_gap = row_line[:, cut] - row_here
                col_gap = col_line[:, cut] - col_here
                square = row_gap * row_gap + col_gap * col_gap
                if n == 0:
                    distance = square * lax.rsqrt(jnp.maximum(square, 1e-30))
                else:
                    distance = square * lax.rsqrt(square)
                fading = jnp.maximum(unit - distance, 0.0)
                fading = fading * fading
                fading = fading * fading
                decay = jnp.exp2(distance * (-ratio * LOG2E / unit))
                lead = (distance + unit / ratio) * (distance + unit / 4.0)
                kernel = (lead * decay) * fading
                if n == 0:
                    kernel = kernel * (NEIGHBOURS + 1.0)
                high = kernel.astype(jnp.bfloat16)
                low = (kernel - high.astype(F32)).astype(jnp.bfloat16)
                base = n * wide + part * lanes
                tiles[block, i, 0:tile_rows, base : base + lanes] = high
                tiles[block, i, tile_rows : 2 * tile_rows, base : base + lanes] = low
        return carry

    steps = BLOCKS_DEV * groups
    shares = (0, 8, 20, 32, 40, 52, 64)

    def build_some(part):
        lax.fori_loop(shares[part] * steps // 64, shares[part + 1] * steps // 64, build_tile, 0)

    m_copies = exchange_copies(staged_m, recv_m, ns, exch_s.at[3], exch_r.at[3])
    edge_value = HUBER_EDGE
    for sweep in range(SWEEPS):
        row_buf = (row_buf0, row_buf1)[min(sweep, 1)]
        col_send = (col_send0, col_send1)[min(sweep, 1)]
        col_got = (col_got0, col_got1)[min(sweep, 1)]
        col_all = (col_all0, col_all1)[min(sweep, 1)]

        def clipped(r):
            value = (obs[r] - row_eff[pl.ds(r, 1)] - col_eff[...]) * inv
            return weight[r] * jnp.clip(value, -edge_value, edge_value)

        def row_step(r, carry):
            row_buf[0, pl.ds(r, 1)] = jnp.sum(clipped(r), axis=0, keepdims=True)
            if sweep == 0:
                row_buf[0, pl.ds(rows + r, 1)] = jnp.sum(weight[r], axis=0, keepdims=True)
            return carry

        lax.fori_loop(0, rows, row_step, 0)
        sums = spread_copies(row_buf, "wide", nw, sem_s.at[sweep], sem_r.at[sweep])
        start(sums)
        if sweep == 0:
            wait(place_copies)
            prepare_places()
        build_some(3 * sweep)
        wait(sums)
        total = gathered_sum(row_buf, "wide", nw)
        if sweep == 0:
            row_cnt[...] = jnp.maximum(total[rows:], 1.0)
        row_eff[...] = row_eff[...] + scale[...] * total[:rows] / row_cnt[...]
        if sweep == SWEEPS - 1:
            start(row_copies)

            def describe(k, carry):
                for pair in range(pairs):
                    staged_m[k, pair : pair + 1] = row_eff[pl.ds(chosen[k] * pairs + pair, 1)]
                for r in range(strip_rows):
                    at = pairs + r
                    staged_m[k, at : at + 1] = place[2, pl.ds(row_reach + chosen[k] * strip_rows + r, 1)]
                return carry

            staged_m[...] = jnp.zeros_like(staged_m)
            lax.fori_loop(0, ns, describe, 0)
            start(m_copies)

        def col_step(r, carry):
            return carry + clipped(r)

        part = fold(lax.fori_loop(0, rows, col_step, jnp.zeros(full, F32)))
        col_part[0:half] = beside(part[:half], part[half:])
        count = jnp.sum(seen, axis=0, keepdims=True)
        for k in range(ns):
            owner_of = lax.rem(me + k, ns)
            col_send[k, 0:chunk] = col_part[pl.ds(pl.multiple_of(owner_of * chunk, chunk), chunk)]
            col_send[k, chunk : chunk + 8] = jnp.broadcast_to(count, (8, cols))
        col_got[0] = col_send[0]
        sums = [
            remote(
                col_send.at[k], col_got.at[k],
                sem_s.at[2 + sweep, k], sem_r.at[2 + sweep, k], "sixteen", ns, k,
            )
            for k in range(1, ns)
        ]
        start(sums)
        start(bulk[2 * sweep + 1])
        build_some(3 * sweep + 1)
        wait(sums)
        total = gathered_sum(col_got, "sixteen", ns)
        col_all[0] = total[:chunk]
        if sweep == 0:
            counts = jnp.broadcast_to(total[chunk : chunk + 1], full).T
            col_cnt[...] = jnp.maximum(counts, 1.0)
        sums = spread_copies(col_all, "sixteen", ns, sem_s.at[9 + sweep], sem_r.at[9 + sweep])
        start(sums)
        start(bulk[2 * sweep + 2])
        build_some(3 * sweep + 2)
        wait(sums)
        total = jnp.concatenate(
            [col_all[lax.rem(me - o + ns, ns)] for o in range(ns)], axis=0
        )
        y = total[:half]
        z = swap(y)
        both = jnp.concatenate([beside(y, z), beside(z, y)], axis=0)
        col_eff[...] = col_eff[...] + scale[...] * both / col_cnt[...]

    for copies in obs_copies:
        wait(copies)

    def remain(r, carry):
        obs[r] = weight[r] * (obs[r] - row_eff[pl.ds(r, 1)] - col_eff[...])
        return carry

    lax.fori_loop(0, rows, remain, 0)
    p = obs

    def windows(source, first, h):
        for pair in range(pairs):
            x = source[first + pair]
            z = swap(x)
            low = low_lanes(x)
            for parity in range(2):
                y = jnp.where(low, x, z) if parity == 0 else jnp.where(low, z, x)
                high = y.astype(jnp.bfloat16).astype(F32)
                both = jnp.where(low, high, y - high)
                win[0, h, 2 * pair + parity] = both.astype(jnp.bfloat16)
                win[1, h, 2 * pair + parity, 0 : cols - GROUP] = both[
                    GROUP // 2 : cols - GROUP // 2
                ].astype(jnp.bfloat16)

    def own_windows(source):
        def one(b, carry):
            windows(source, b * pairs, REACH + b)
            return carry

        lax.fori_loop(0, BLOCKS_DEV, one, 0)

    def edge_windows(source):
        def one(b, carry):
            windows(source, b * pairs, b)
            windows(source, reach + b * pairs, REACH + BLOCKS_DEV + b)
            return carry

        lax.fori_loop(0, REACH, one, 0)

    own_windows(p)
    wait(row_copies)
    seen_t = turned(place[2], lanes)
    for t in range(reach):
        for at, r in ((t, t), (reach + t, reach + rows + t)):
            there = beside(across(seen_t, 2 * r, full), across(seen_t, 2 * r + 1, full))
            edge[at] = there * (edge[at] - row_edge[pl.ds(at, 1)] - col_eff[...])
    edge_windows(edge)
    dots[...] = jnp.zeros_like(dots)

    def apply(block, own_of, store):
        for i, s in enumerate(starts):
            shifted = (s % GROUP) // (GROUP // 2)
            base = s - shifted * (GROUP // 2)
            acc = jnp.zeros((2 * tile_rows, lanes), F32)
            for n in range(NEIGHBOURS + 1):
                h = block + REACH + offs[n]
                acc = acc + jnp.dot(
                    tiles[block, i, :, n * wide : (n + 1) * wide],
                    win[shifted, h, :, base : base + span, :].reshape(wide, lanes),
                    preferred_element_type=F32,
                )
            y = fold(acc[:tile_rows] + acc[tile_rows:])
            for pair in range(pairs):
                even = y[(2 * pair) * GROUP : (2 * pair + 1) * GROUP]
                odd = y[(2 * pair + 1) * GROUP : (2 * pair + 2) * GROUP]
                own = own_of(pair, i * GROUP)
                store(pair, i * GROUP, own, NUGGET_TERM * own + beside(even, odd))

    def gather_dot(k, x, y):
        z = x * y
        dots[k] = dots[k] + (z[: GROUP // 2] + z[GROUP // 2 :])

    def q_copies(t):
        return halo_copies(q, q_edge, pairs, halo_s, halo_r, t)

    def first_block(block):
        def own_of(pair, at):
            return p[block * pairs + pair, at : at + GROUP, :]

        def store(pair, at, own, value):
            q[block * pairs + pair, at : at + GROUP, :] = value
            gather_dot(0, own, own)
            gather_dot(1, own, value)
            gather_dot(2, value, value)

        apply(block, own_of, store)

    def first_pass(t, carry):
        def one(side, inner):
            first_block(side * REACH + t)
            return inner

        lax.fori_loop(0, 2, one, 0)
        start(q_copies(t))
        return carry

    lax.fori_loop(0, REACH, first_pass, 0)

    stage(staged_q, q)
    q_exchange = exchange_copies(staged_q, recv_q, ns, exch_s.at[1], exch_r.at[1])
    start(q_exchange[0::2])
    own_windows(q)
    wait(p_copies)
    wait(m_copies)
    facts = turned(recv_m[...].reshape(ns * 8, cols), lanes)
    for k in range(ns):
        for pair in range(pairs):
            at = 8 * k + pairs + 2 * pair
            there = beside(across(facts, at, full), across(facts, at + 1, full))
            recv_p[k, pair] = there * (recv_p[k, pair] - recv_m[k, pair : pair + 1] - col_eff[...])
    for t in range(REACH):
        wait(q_copies(t))
    start(q_exchange[1::2])
    edge_windows(q_edge)

    w_copies = exchange_copies(staged_w, recv_w, ns, exch_s.at[2], exch_r.at[2])
    one_each = ns == BLOCKS_DEV
    held = 1 + ns // 2 if one_each else 0

    def second_block(g, carry):
        slot = lax.rem(g + 1, BLOCKS_DEV)
        block = chosen[slot] if one_each else g

        def own_of(pair, at):
            return q[block * pairs + pair, at : at + GROUP, :]

        def store(pair, at, own, value):
            gather_dot(3, own, value)
            if one_each:
                staged_w[slot, pair, at : at + GROUP, :] = value
            else:
                edge[g * pairs + pair, at : at + GROUP, :] = value

        apply(block, own_of, store)
        if one_each:
            for k in range(1, held):

                @pl.when(g == k - 1)
                def _(k=k):
                    w_copies[k].start()

        return carry

    lax.fori_loop(0, BLOCKS_DEV, second_block, 0)
    if not one_each:
        stage(staged_w, edge)

    for k in range(4):
        dot_w[0, k : k + 1] = jnp.sum(fold(dots[k]), axis=0, keepdims=True)
    dot_w[0, 4:8] = jnp.zeros((4, lanes), F32)
    sums = spread_copies(dot_w, "wide", nw, sem_s.at[4], sem_r.at[4])
    start(sums)
    wait(sums)
    dot_s[0] = gathered_sum(dot_w, "wide", nw)
    sums = spread_copies(dot_s, "sixteen", ns, sem_s.at[5], sem_r.at[5])
    start(sums)
    start((w_copies[:1] if one_each else []) + w_copies[held:])
    wait(sums)
    total = gathered_sum(dot_s, "sixteen", ns)
    m0, m1, m2, m3 = (total[k : k + 1] for k in range(4))
    alpha = m0 / m1
    norm = (m0 - 2.0 * alpha * m1) + alpha * alpha * m2
    grown = 1.0 + norm / m0
    bend = grown * (grown * m1 - 2.0 * alpha * m2) + alpha * alpha * m3
    second = norm / bend
    near = alpha + second * grown
    far = second * alpha

    def slot_of(j):
        return lax.rem(me - j + ns, ns) if static_came else came[j]

    def put(target, source):
        for j in range(BLOCKS_DEV):
            k = slot_of(j)
            for pair in range(pairs):
                value = source[k, pair]
                for parity in range(2):
                    at = (2 * pair + parity) * cols
                    target[:, j, at : at + cols] = value[parity * fields : (parity + 1) * fields]

    wait(q_exchange)
    for k in range(ns):
        for pair in range(pairs):
            staged_q[k, pair] = (near * recv_p[k, pair] - far * recv_q[k, pair]).T
            recv_p[k, pair] = recv_p[k, pair] - near * recv_q[k, pair]
    put(out, staged_q)
    for k in range(ns):
        wait(w_copies[k : k + 1])
        for pair in range(pairs):
            recv_w[k, pair] = (recv_p[k, pair] + far * recv_w[k, pair]).T
    put(rest, recv_w)


def owned_table(group_map, owners, per_owner):
    total_strips = group_map.shape[0]
    member = (group_map[None, :] == jnp.arange(owners, dtype=jnp.int32)[:, None]).astype(jnp.int32)
    ranked = jnp.cumsum(member, axis=1, dtype=jnp.int32) - 1
    slot_hit = (ranked[:, :, None] == jnp.arange(per_owner, dtype=jnp.int32)[None, None, :]).astype(
        jnp.int32
    ) * member[:, :, None]
    numbers = jnp.arange(total_strips, dtype=jnp.int32)
    return jnp.sum(slot_hit * numbers[None, :, None], axis=1, dtype=jnp.int32)


def on_device(observations, huber_scale, observed, jitter, owner_map, neighbours):
    fields, row_dev, col_dev = observations.shape
    nw, ns = lax.axis_size("wide"), lax.axis_size("sixteen")
    strip_rows = BLOCK // col_dev
    rows, lanes = row_dev // 2, 2 * fields
    pairs = strip_rows // 2
    reach = REACH * pairs
    shape = jax.ShapeDtypeStruct

    cut = 6 * strip_rows
    span = GROUP + 2 * cut
    starts = tuple(
        min(max(GROUP * i - cut, 0), col_dev - span) for i in range(col_dev // GROUP)
    )
    groups = len(starts)
    wide = strip_rows * span
    blocks_halo = BLOCKS_DEV + 2 * REACH

    static_came = ns == BLOCKS_DEV
    if static_came:
        came = owner_map
    else:
        my_place = lax.axis_index("sixteen")
        table = owned_table(owner_map[0], ns, BLOCKS_DEV)
        my_ids = lax.dynamic_index_in_dim(table, my_place, 0, keepdims=False)
        came = (my_place - my_ids // BLOCKS_DEV + ns) % ns

    most = max(nw, ns)
    vm = lambda *s: pltpu.VMEM(s, F32)
    moved = (ns, pairs, col_dev, lanes)
    piece = (ns, col_dev // 2 // ns + 8, lanes)
    field = (rows, col_dev, lanes)
    place_rows = row_dev + 4 * reach
    out_shape = shape((fields, BLOCKS_DEV, BLOCK), F32)
    solution_now, residual_now = pl.pallas_call(
        functools.partial(solve_kernel, nw, ns, fields, strip_rows, starts, span, static_came),
        out_shape=(out_shape, out_shape),
        in_specs=[SMEM] * 3 + [VMEM] * 4,
        out_specs=(VMEM, VMEM),
        scratch_shapes=[
            pltpu.SMEM((NEIGHBOURS + 1,), jnp.int32),
            pltpu.SMEM((ns,), jnp.int32),
            vm(*field), vm(*field), vm(2 * reach, col_dev, lanes), vm(*field),
            vm(2 * reach, col_dev, lanes),
            vm(*moved), vm(*moved), vm(*moved), vm(*moved), vm(*moved), vm(*moved),
            vm(ns, 8, lanes), vm(ns, 8, lanes),
            pltpu.VMEM((BLOCKS_DEV, groups, 2 * strip_rows * GROUP, (NEIGHBOURS + 1) * wide), jnp.bfloat16),
            pltpu.VMEM((2, blocks_halo, strip_rows, col_dev, lanes), jnp.bfloat16),
            vm(2, row_dev, col_dev, lanes),
            vm(groups, 2, blocks_halo, wide),
            vm(3, place_rows, col_dev),
            vm(2, place_rows, col_dev),
            vm(1, lanes),
            vm(rows, lanes), vm(rows, lanes), vm(col_dev, lanes), vm(col_dev, lanes),
            vm(2 * reach, lanes),
            vm(nw, 2 * rows, lanes), vm(nw, rows, lanes),
            vm(col_dev // 2, lanes),
            vm(*piece), vm(*piece), vm(*piece), vm(*piece),
            vm(ns, col_dev // 2 // ns, lanes), vm(ns, col_dev // 2 // ns, lanes),
            vm(4, 8, lanes), vm(nw, 8, lanes), vm(ns, 8, lanes),
            pltpu.SemaphoreType.DMA((11, most)), pltpu.SemaphoreType.DMA((11, most)),
            pltpu.SemaphoreType.DMA((4, ns)), pltpu.SemaphoreType.DMA((4, ns)),
            pltpu.SemaphoreType.DMA((2, reach)), pltpu.SemaphoreType.DMA((2, reach)),
            pltpu.SemaphoreType.DMA((2, REACH)), pltpu.SemaphoreType.DMA((2, REACH)),
        ],
        compiler_params=pltpu.CompilerParams(
            collective_id=0, has_side_effects=True, vmem_limit_bytes=57 * 1000 * 1000 if static_came else 66 * 1000 * 1000
        ),
    )(
        owner_map,
        jnp.transpose(neighbours, (2, 0, 1)),
        came,
        observations.reshape(fields * row_dev, col_dev),
        huber_scale.reshape(1, fields),
        observed,
        jitter,
    )
    return solution_now[None, None], residual_now[None, None]


def solution(mesh):
    return jax.shard_map(
        on_device,
        mesh=mesh,
        in_specs=(
            P(None, "sixteen", "wide"),
            P(),
            P("sixteen", "wide"),
            P(None, "sixteen", "wide"),
            P("wide", None),
            P("wide", None, None),
        ),
        out_specs=(P("wide", "sixteen", None, None, None), P("wide", "sixteen", None, None, None)),
        check_vma=False,
    )
```

```python
import functools

import jax
import jax.numpy as jnp
from jax import lax
from jax.experimental import pallas as pl
from jax.experimental.pallas import tpu as pltpu
from jax.sharding import PartitionSpec as P

BLOCK = 512
BLOCKS_DEV = 8
REACH = 4
NEIGHBOURS = 6
SWEEPS = 2

HUBER_EDGE = 1.345
NUGGET_TERM = 1.0
SILL_TERM = 0.02
ROOT_THREE = 1.7320508075688772
LOG2E = 1.4426950408889634
GROUP = 16
MESH = pl.DeviceIdType.MESH
VMEM = pl.BlockSpec(memory_space=pltpu.VMEM)
SMEM = pl.BlockSpec(memory_space=pltpu.SMEM)
F32 = jnp.float32


def say_hello(sizes):
    barrier = pltpu.get_barrier_semaphore()
    for axis, n in sizes:
        me = lax.axis_index(axis)

        def say(k, carry, axis=axis, n=n, me=me):
            pl.semaphore_signal(
                barrier, inc=1, device_id={axis: lax.rem(me + k, n)}, device_id_type=MESH
            )
            return carry

        lax.fori_loop(1, n, say, 0)


def hear_hello(sizes):
    pl.semaphore_wait(pltpu.get_barrier_semaphore(), sum(n - 1 for _, n in sizes))


def remote(src, dst, send, recv, axis, n, shift):
    return pltpu.make_async_remote_copy(
        src_ref=src,
        dst_ref=dst,
        send_sem=send,
        recv_sem=recv,
        device_id={axis: lax.rem(lax.axis_index(axis) + shift, n)},
        device_id_type=MESH,
    )


def start(copies):
    for c in copies:
        c.start()


def wait(copies):
    for c in copies:
        c.wait()


def spread_copies(buffer, axis, n, send, recv):
    return [
        remote(buffer.at[0], buffer.at[k], send.at[k], recv.at[k], axis, n, k) for k in range(1, n)
    ]


def gathered_sum(buffer, axis, n):
    me = lax.axis_index(axis)
    total = None
    for owner in range(n):
        term = buffer[lax.rem(me - owner + n, n)]
        total = term if total is None else total + term
    return total


def exchange_copies(staged, received, n, send, recv):
    return [pltpu.make_async_copy(staged.at[0], received.at[0], send.at[0])] + [
        remote(staged.at[k], received.at[k], send.at[k], recv.at[k], "sixteen", n, k)
        for k in range(1, n)
    ]


def edge_copies(source, target, reach, n, send, recv):
    rows = source.shape[0]
    return [
        remote(
            source.at[pl.ds(first, reach)],
            target.at[pl.ds(side * reach, reach)],
            send.at[side],
            recv.at[side],
            "sixteen",
            n,
            shift,
        )
        for side, first, shift in ((0, rows - reach, 1), (1, 0, n - 1))
    ]


def swap(x):
    return pltpu.roll(x, x.shape[-1] // 2, x.ndim - 1)


def fold(x):
    return x + swap(x)


def low_lanes(x):
    return lax.broadcasted_iota(jnp.int32, x.shape, x.ndim - 1) < x.shape[-1] // 2


def beside(even, odd):
    return jnp.where(low_lanes(even), even, odd)


def turned(x, size):
    rows = x.shape[0]
    if rows < size:
        x = jnp.concatenate([x, jnp.zeros((size - rows, x.shape[1]), x.dtype)], axis=0)
    return x.T


def across(x, k, shape):
    return jnp.broadcast_to(x[:, k : k + 1], shape)


def solve_kernel(
    nw, ns, fields, strip_rows, starts, span, static_came,
    came, owner_hbm, listed_hbm, obs_hbm, scale_hbm, seen_hbm, jitter_hbm,
    out, rest,
    offs, chosen, owner, listed, obs_in, scale_in, seen_in, jitter_in,
    obs, weight, edge, q, q_edge, staged_p, recv_p, staged_q, recv_q, staged_w, recv_w,
    staged_m, recv_m, tiles, win, cb, oth, own_oth, place, coords,
    scale, row_eff, row_cnt, col_eff, col_cnt, row_edge, row_buf0, row_buf1,
    col_part, col_send0, col_send1, col_got0, col_got1, col_all0, col_all1,
    dots, dot_w, dot_s,
    sem_in, sem_s, sem_r, exch_s, exch_r, obs_s, obs_r, halo_s, halo_r,
):
    rows, cols, lanes = obs.shape
    half = cols // 2
    chunk = half // ns
    pairs = strip_rows // 2
    reach = REACH * pairs
    row_dev = 2 * rows
    row_reach = 2 * reach
    groups = len(starts)
    wide = strip_rows * span
    parts = wide // lanes
    tile_rows = strip_rows * GROUP
    total_strips = BLOCKS_DEV * ns
    me = lax.axis_index("sixteen")
    group_me = lax.axis_index("wide")
    everyone = (("wide", nw), ("sixteen", ns))
    full = (cols, lanes)

    say_hello(everyone)
    arrivals = [
        pltpu.make_async_copy(source, target, sem_in.at[k])
        for k, (source, target) in enumerate(
            (
                (obs_hbm, obs_in), (scale_hbm, scale_in), (seen_hbm, seen_in),
                (jitter_hbm, jitter_in), (owner_hbm, owner), (listed_hbm, listed),
            )
        )
    ]
    start(arrivals)
    wait(arrivals)

    def pack(r, carry):
        both = jnp.concatenate(
            [obs_in[pl.ds(2 * r + parity, fields, stride=row_dev), :] for parity in range(2)],
            axis=0,
        )
        obs[r] = both.T
        return carry

    lax.fori_loop(0, rows, pack, 0)

    row_number = lax.broadcasted_iota(jnp.int32, (row_dev, cols), 0) + me * row_dev
    col_number = lax.broadcasted_iota(jnp.int32, (row_dev, cols), 1) + group_me * cols
    seen = seen_in[...].astype(F32)
    place[0, pl.ds(row_reach, row_dev)] = row_number.astype(F32) + jitter_in[0]
    place[1, pl.ds(row_reach, row_dev)] = col_number.astype(F32) + jitter_in[1]
    place[2, pl.ds(row_reach, row_dev)] = seen

    for n in range(NEIGHBOURS):
        other = listed[n, 0, 0]
        offs[n + 1] = jnp.where(other < total_strips // 2, other, other - total_strips)
    offs[0] = 0
    for k in range(ns):
        target = lax.rem(me + k, ns)
        pick = 0
        for j in range(BLOCKS_DEV):
            pick = jnp.where(owner[0, me * BLOCKS_DEV + j] == target, j, pick)
        chosen[k] = pick

    hear_hello(everyone)
    place_copies = [
        remote(
            place.at[:, pl.ds(row_dev, row_reach)],
            place.at[:, pl.ds(0, row_reach)],
            sem_s.at[6, 0], sem_r.at[6, 0], "sixteen", ns, 1,
        ),
        remote(
            place.at[:, pl.ds(row_reach, row_reach)],
            place.at[:, pl.ds(row_reach + row_dev, row_reach)],
            sem_s.at[6, 1], sem_r.at[6, 1], "sixteen", ns, ns - 1,
        ),
    ]

    def halo_copies(source, target, size, send, recv, t):
        return [
            remote(
                source.at[pl.ds(rows - reach + t * size, size)],
                target.at[pl.ds(t * size, size)],
                send.at[0, t], recv.at[0, t], "sixteen", ns, 1,
            ),
            remote(
                source.at[pl.ds(t * size, size)],
                target.at[pl.ds(reach + t * size, size)],
                send.at[1, t], recv.at[1, t], "sixteen", ns, ns - 1,
            ),
        ]

    obs_copies = [halo_copies(obs, edge, 1, obs_s, obs_r, t) for t in range(reach)]
    row_copies = edge_copies(row_eff, row_edge, reach, ns, sem_s.at[8], sem_r.at[8])
    start(place_copies)

    def stage(staged, source):
        def one(k, carry):
            for pair in range(pairs):
                staged[k, pair] = source[chosen[k] * pairs + pair]
            return carry

        lax.fori_loop(0, ns, one, 0)

    stage(staged_p, obs)
    p_copies = exchange_copies(staged_p, recv_p, ns, exch_s.at[0], exch_r.at[0])

    near_first = p_copies[2::2]
    bulk = [
        p_copies[:1] + sum(obs_copies[0:3], []) + near_first[0::3],
        sum(obs_copies[3:4], []),
        sum(obs_copies[4:6], []) + near_first[1::3],
        sum(obs_copies[6:7], []),
        sum(obs_copies[7:8], []) + near_first[2::3] + p_copies[1::2],
    ]
    start(bulk[0])
    seen_t = turned(seen, lanes)
    for r in range(rows):
        weight[r] = beside(across(seen_t, 2 * r, full), across(seen_t, 2 * r + 1, full))
    one_scale = scale_in[...]
    scale[...] = jnp.concatenate([one_scale, one_scale], axis=1)
    inv = 1.0 / scale[...]
    row_eff[...] = jnp.zeros_like(row_eff)
    col_eff[...] = jnp.zeros_like(col_eff)

    spread = 2.0 * strip_rows
    cutoff = 6.0 * strip_rows
    ratio = ROOT_THREE * cutoff / spread
    unit = (4.0 * ratio * SILL_TERM) ** (1.0 / 6.0)

    def centred(first, count):
        at = pl.ds(first, count)
        coords[0, at] = (place[0, at] - (me * row_dev + row_dev // 2).astype(F32)) * (unit / cutoff)
        coords[1, at] = (place[1, at] - (group_me * cols + cols // 2).astype(F32)) * (unit / cutoff)

    def lines(target, first, blocks):
        for c in range(2):
            for pair in range(pairs):
                a = [
                    coords[c, pl.ds(first + 2 * pair + parity, blocks, stride=strip_rows), :]
                    for parity in range(2)
                ]
                for i, s in enumerate(starts):
                    x = pltpu.roll(a[0], (cols - s) % cols, 1)
                    y = pltpu.roll(a[1], (cols + span - s) % cols, 1)
                    target[i, c, :, pair * lanes : (pair + 1) * lanes] = beside(x, y)

    def prepare_own():
        centred(row_reach, row_dev)
        for c in range(2):
            t = turned(coords[c, pl.ds(row_reach, row_dev)], lanes)
            for r in range(row_dev):
                cb[c, r] = across(t, r, full)
        lines(own_oth, row_reach, BLOCKS_DEV)

    def prepare_all():
        centred(0, row_reach)
        centred(row_reach + row_dev, row_reach)
        lines(oth, 0, oth.shape[2])

    def tile_builder(source, first_block, members):
        def build(t, carry):
            block, i = t // groups, lax.rem(t, groups)
            at = pl.multiple_of(i * GROUP, GROUP)
            first = pl.multiple_of(block * strip_rows, strip_rows)
            row_here = cb[0, pl.ds(first, strip_rows), pl.ds(at, GROUP), :].reshape(tile_rows, lanes)
            col_here = cb[1, pl.ds(first, strip_rows), pl.ds(at, GROUP), :].reshape(tile_rows, lanes)
            for n in members:
                h = block + first_block + (offs[n] if n else 0)
                row_line = source[i, 0, pl.ds(h, 1), :]
                col_line = source[i, 1, pl.ds(h, 1), :]
                for part in range(parts):
                    cut = slice(part * lanes, (part + 1) * lanes)
                    row_gap = row_line[:, cut] - row_here
                    col_gap = col_line[:, cut] - col_here
                    square = row_gap * row_gap + col_gap * col_gap
                    if n == 0:
                        distance = square * lax.rsqrt(jnp.maximum(square, 1e-30))
                    else:
                        distance = square * lax.rsqrt(square)
                    fading = jnp.maximum(unit - distance, 0.0)
                    fading = fading * fading
                    fading = fading * fading
                    decay = jnp.exp2(distance * (-ratio * LOG2E / unit))
                    lead = (distance + unit / ratio) * (distance + unit / 4.0)
                    kernel = (lead * decay) * fading
                    if n == 0:
                        kernel = kernel * (NEIGHBOURS + 1.0)
                    high = kernel.astype(jnp.bfloat16)
                    low = (kernel - high.astype(F32)).astype(jnp.bfloat16)
                    tiles[block, i, parts * n + part, 0:tile_rows] = high
                    tiles[block, i, parts * n + part, tile_rows : 2 * tile_rows] = low
            return carry

        return build

    build_own = tile_builder(own_oth, 0, (0,))
    build_tile = tile_builder(oth, REACH, tuple(range(1, NEIGHBOURS + 1)))

    steps = BLOCKS_DEV * groups
    shares = (0, 9, 20, 32, 41, 52, 64)

    def build_some(part):
        lax.fori_loop(shares[part] * steps // 64, shares[part + 1] * steps // 64, build_tile, 0)

    m_copies = exchange_copies(staged_m, recv_m, ns, exch_s.at[3], exch_r.at[3])
    edge_value = HUBER_EDGE
    for sweep in range(SWEEPS):
        row_buf = (row_buf0, row_buf1)[min(sweep, 1)]
        col_send = (col_send0, col_send1)[min(sweep, 1)]
        col_got = (col_got0, col_got1)[min(sweep, 1)]
        col_all = (col_all0, col_all1)[min(sweep, 1)]

        def clipped(r):
            value = (obs[r] - row_eff[pl.ds(r, 1)] - col_eff[...]) * inv
            return weight[r] * jnp.clip(value, -edge_value, edge_value)

        def row_step(r, carry):
            row_buf[0, pl.ds(r, 1)] = jnp.sum(clipped(r), axis=0, keepdims=True)
            if sweep == 0:
                row_buf[0, pl.ds(rows + r, 1)] = jnp.sum(weight[r], axis=0, keepdims=True)
            return carry

        lax.fori_loop(0, rows, row_step, 0)
        sums = spread_copies(row_buf, "wide", nw, sem_s.at[sweep], sem_r.at[sweep])
        start(sums)
        if sweep == 0:
            prepare_own()
            lax.fori_loop(0, steps, build_own, 0)
            wait(place_copies)
            prepare_all()
        build_some(3 * sweep)
        wait(sums)
        total = gathered_sum(row_buf, "wide", nw)
        if sweep == 0:
            row_cnt[...] = jnp.maximum(total[rows:], 1.0)
        row_eff[...] = row_eff[...] + scale[...] * total[:rows] / row_cnt[...]
        if sweep == SWEEPS - 1:
            start(row_copies)

            def describe(k, carry):
                for pair in range(pairs):
                    staged_m[k, pair : pair + 1] = row_eff[pl.ds(chosen[k] * pairs + pair, 1)]
                for r in range(strip_rows):
                    at = pairs + r
                    staged_m[k, at : at + 1] = place[2, pl.ds(row_reach + chosen[k] * strip_rows + r, 1)]
                return carry

            staged_m[...] = jnp.zeros_like(staged_m)
            lax.fori_loop(0, ns, describe, 0)
            start(m_copies)

        def col_step(r, carry):
            return carry + clipped(r)

        part = fold(lax.fori_loop(0, rows, col_step, jnp.zeros(full, F32)))
        col_part[0:half] = beside(part[:half], part[half:])
        count = jnp.sum(seen, axis=0, keepdims=True)
        for k in range(ns):
            owner_of = lax.rem(me + k, ns)
            col_send[k, 0:chunk] = col_part[pl.ds(pl.multiple_of(owner_of * chunk, chunk), chunk)]
            col_send[k, chunk : chunk + 8] = jnp.broadcast_to(count, (8, cols))
        col_got[0] = col_send[0]
        sums = [
            remote(
                col_send.at[k], col_got.at[k],
                sem_s.at[2 + sweep, k], sem_r.at[2 + sweep, k], "sixteen", ns, k,
            )
            for k in range(1, ns)
        ]
        start(sums)
        start(bulk[2 * sweep + 1])
        build_some(3 * sweep + 1)
        wait(sums)
        total = gathered_sum(col_got, "sixteen", ns)
        col_all[0] = total[:chunk]
        if sweep == 0:
            counts = jnp.broadcast_to(total[chunk : chunk + 1], full).T
            col_cnt[...] = jnp.maximum(counts, 1.0)
        sums = spread_copies(col_all, "sixteen", ns, sem_s.at[9 + sweep], sem_r.at[9 + sweep])
        start(sums)
        start(bulk[2 * sweep + 2])
        build_some(3 * sweep + 2)
        wait(sums)
        total = jnp.concatenate(
            [col_all[lax.rem(me - o + ns, ns)] for o in range(ns)], axis=0
        )
        y = total[:half]
        z = swap(y)
        both = jnp.concatenate([beside(y, z), beside(z, y)], axis=0)
        col_eff[...] = col_eff[...] + scale[...] * both / col_cnt[...]

    for copies in obs_copies:
        wait(copies)

    def remain(r, carry):
        obs[r] = weight[r] * (obs[r] - row_eff[pl.ds(r, 1)] - col_eff[...])
        return carry

    lax.fori_loop(0, rows, remain, 0)
    p = obs

    def windows(source, first, h):
        for pair in range(pairs):
            x = source[first + pair]
            z = swap(x)
            low = low_lanes(x)
            for parity in range(2):
                y = jnp.where(low, x, z) if parity == 0 else jnp.where(low, z, x)
                high = y.astype(jnp.bfloat16).astype(F32)
                both = jnp.where(low, high, y - high)
                win[0, h, 2 * pair + parity] = both.astype(jnp.bfloat16)
                win[1, h, 2 * pair + parity, 0 : cols - GROUP] = both[
                    GROUP // 2 : cols - GROUP // 2
                ].astype(jnp.bfloat16)

    def own_windows(source):
        def one(b, carry):
            windows(source, b * pairs, REACH + b)
            return carry

        lax.fori_loop(0, BLOCKS_DEV, one, 0)

    def edge_windows(source):
        def one(b, carry):
            windows(source, b * pairs, b)
            windows(source, reach + b * pairs, REACH + BLOCKS_DEV + b)
            return carry

        lax.fori_loop(0, REACH, one, 0)

    own_windows(p)
    wait(row_copies)
    seen_t = turned(place[2], lanes)
    for t in range(reach):
        for at, r in ((t, t), (reach + t, reach + rows + t)):
            there = beside(across(seen_t, 2 * r, full), across(seen_t, 2 * r + 1, full))
            edge[at] = there * (edge[at] - row_edge[pl.ds(at, 1)] - col_eff[...])
    edge_windows(edge)
    dots[...] = jnp.zeros_like(dots)

    def apply(block, own_of, store):
        for i, s in enumerate(starts):
            shifted = (s % GROUP) // (GROUP // 2)
            base = s - shifted * (GROUP // 2)
            acc = jnp.zeros((2 * tile_rows, lanes), F32)
            for n in range(NEIGHBOURS + 1):
                h = block + REACH + offs[n]
                acc = acc + jnp.dot(
                    jnp.concatenate(
                        [tiles[block, i, parts * n + part] for part in range(parts)], axis=1
                    ),
                    win[shifted, h, :, base : base + span, :].reshape(wide, lanes),
                    preferred_element_type=F32,
                )
            y = fold(acc[:tile_rows] + acc[tile_rows:])
            for pair in range(pairs):
                even = y[(2 * pair) * GROUP : (2 * pair + 1) * GROUP]
                odd = y[(2 * pair + 1) * GROUP : (2 * pair + 2) * GROUP]
                own = own_of(pair, i * GROUP)
                store(pair, i * GROUP, own, NUGGET_TERM * own + beside(even, odd))

    def gather_dot(k, x, y):
        z = x * y
        dots[k] = dots[k] + (z[: GROUP // 2] + z[GROUP // 2 :])

    def q_copies(t):
        return halo_copies(q, q_edge, pairs, halo_s, halo_r, t)

    def first_block(block):
        def own_of(pair, at):
            return p[block * pairs + pair, at : at + GROUP, :]

        def store(pair, at, own, value):
            q[block * pairs + pair, at : at + GROUP, :] = value
            gather_dot(0, own, own)
            gather_dot(1, own, value)
            gather_dot(2, value, value)

        apply(block, own_of, store)

    def first_pass(u, carry):
        t, side = u // 2, lax.rem(u, 2)
        first_block(side * REACH + t)
        up, down = q_copies(t)

        @pl.when(side == 0)
        def _():
            down.start()

        @pl.when(side == 1)
        def _():
            up.start()

        return carry

    lax.fori_loop(0, BLOCKS_DEV, first_pass, 0)

    stage(staged_q, q)
    q_exchange = exchange_copies(staged_q, recv_q, ns, exch_s.at[1], exch_r.at[1])
    start(q_exchange[0::2])
    own_windows(q)
    wait(p_copies)
    wait(m_copies)
    facts = turned(recv_m[...].reshape(ns * 8, cols), lanes)
    for k in range(ns):
        for pair in range(pairs):
            at = 8 * k + pairs + 2 * pair
            there = beside(across(facts, at, full), across(facts, at + 1, full))
            recv_p[k, pair] = there * (recv_p[k, pair] - recv_m[k, pair : pair + 1] - col_eff[...])
    for t in range(REACH):
        wait(q_copies(t))
    start(q_exchange[1::2])
    edge_windows(q_edge)

    w_copies = exchange_copies(staged_w, recv_w, ns, exch_s.at[2], exch_r.at[2])
    one_each = ns == BLOCKS_DEV
    held = 3 if one_each else 0

    def second_block(g, carry):
        slot = lax.rem(g + 1, BLOCKS_DEV)
        block = chosen[slot] if one_each else g

        def own_of(pair, at):
            return q[block * pairs + pair, at : at + GROUP, :]

        def store(pair, at, own, value):
            gather_dot(3, own, value)
            if one_each:
                staged_w[slot, pair, at : at + GROUP, :] = value
            else:
                edge[g * pairs + pair, at : at + GROUP, :] = value

        apply(block, own_of, store)
        if one_each:
            for k in range(1, held):

                @pl.when(g == k - 1)
                def _(k=k):
                    w_copies[k].start()

        return carry

    lax.fori_loop(0, BLOCKS_DEV, second_block, 0)
    if not one_each:
        stage(staged_w, edge)

    for k in range(4):
        dot_w[0, k : k + 1] = jnp.sum(fold(dots[k]), axis=0, keepdims=True)
    dot_w[0, 4:8] = jnp.zeros((4, lanes), F32)
    sums = spread_copies(dot_w, "wide", nw, sem_s.at[4], sem_r.at[4])
    start(sums)
    wait(sums)
    dot_s[0] = gathered_sum(dot_w, "wide", nw)
    sums = spread_copies(dot_s, "sixteen", ns, sem_s.at[5], sem_r.at[5])
    start(sums)
    start((w_copies[:1] if one_each else []) + w_copies[held:])
    wait(sums)
    total = gathered_sum(dot_s, "sixteen", ns)
    m0, m1, m2, m3 = (total[k : k + 1] for k in range(4))
    alpha = m0 / m1
    norm = (m0 - 2.0 * alpha * m1) + alpha * alpha * m2
    grown = 1.0 + norm / m0
    bend = grown * (grown * m1 - 2.0 * alpha * m2) + alpha * alpha * m3
    second = norm / bend
    near = alpha + second * grown
    far = second * alpha

    def slot_of(j):
        return lax.rem(me - j + ns, ns) if static_came else came[j]

    def put(target, source):
        for j in range(BLOCKS_DEV):
            k = slot_of(j)
            for pair in range(pairs):
                value = source[k, pair]
                for parity in range(2):
                    at = (2 * pair + parity) * cols
                    target[:, j, at : at + cols] = value[parity * fields : (parity + 1) * fields]

    wait(q_exchange)
    for k in range(ns):
        for pair in range(pairs):
            staged_q[k, pair] = (near * recv_p[k, pair] - far * recv_q[k, pair]).T
            recv_p[k, pair] = recv_p[k, pair] - near * recv_q[k, pair]
    put(out, staged_q)
    for k in range(ns):
        wait(w_copies[k : k + 1])
        for pair in range(pairs):
            recv_w[k, pair] = (recv_p[k, pair] + far * recv_w[k, pair]).T
    put(rest, recv_w)


def owned_table(group_map, owners, per_owner):
    total_strips = group_map.shape[0]
    member = (group_map[None, :] == jnp.arange(owners, dtype=jnp.int32)[:, None]).astype(jnp.int32)
    ranked = jnp.cumsum(member, axis=1, dtype=jnp.int32) - 1
    slot_hit = (ranked[:, :, None] == jnp.arange(per_owner, dtype=jnp.int32)[None, None, :]).astype(
        jnp.int32
    ) * member[:, :, None]
    numbers = jnp.arange(total_strips, dtype=jnp.int32)
    return jnp.sum(slot_hit * numbers[None, :, None], axis=1, dtype=jnp.int32)


def on_device(observations, huber_scale, observed, jitter, owner_map, neighbours):
    fields, row_dev, col_dev = observations.shape
    nw, ns = lax.axis_size("wide"), lax.axis_size("sixteen")
    strip_rows = BLOCK // col_dev
    rows, lanes = row_dev // 2, 2 * fields
    pairs = strip_rows // 2
    reach = REACH * pairs
    shape = jax.ShapeDtypeStruct

    cut = 6 * strip_rows
    span = GROUP + 2 * cut
    starts = tuple(
        min(max(GROUP * i - cut, 0), col_dev - span) for i in range(col_dev // GROUP)
    )
    groups = len(starts)
    wide = strip_rows * span
    blocks_halo = BLOCKS_DEV + 2 * REACH

    static_came = ns == BLOCKS_DEV
    if static_came:
        came = owner_map
    else:
        my_place = lax.axis_index("sixteen")
        table = owned_table(owner_map[0], ns, BLOCKS_DEV)
        my_ids = lax.dynamic_index_in_dim(table, my_place, 0, keepdims=False)
        came = (my_place - my_ids // BLOCKS_DEV + ns) % ns

    most = max(nw, ns)
    anywhere = pl.BlockSpec(memory_space=pl.ANY)
    vm = lambda *s: pltpu.VMEM(s, F32)
    moved = (ns, pairs, col_dev, lanes)
    piece = (ns, col_dev // 2 // ns + 8, lanes)
    field = (rows, col_dev, lanes)
    place_rows = row_dev + 4 * reach
    out_shape = shape((fields, BLOCKS_DEV, BLOCK), F32)
    solution_now, residual_now = pl.pallas_call(
        functools.partial(solve_kernel, nw, ns, fields, strip_rows, starts, span, static_came),
        out_shape=((vm(*out_shape.shape) if static_came else out_shape),) * 2,
        in_specs=[anywhere if static_came else SMEM] + [anywhere] * 6,
        out_specs=(VMEM, VMEM),
        scratch_shapes=[
            pltpu.SMEM((NEIGHBOURS + 1,), jnp.int32),
            pltpu.SMEM((ns,), jnp.int32),
            pltpu.SMEM(owner_map.shape, jnp.int32),
            pltpu.SMEM((NEIGHBOURS, 1, neighbours.shape[1]), jnp.int32),
            vm(fields * row_dev, col_dev),
            vm(1, fields),
            pltpu.VMEM((row_dev, col_dev), jnp.int32),
            vm(2, row_dev, col_dev),
            vm(*field), vm(*field), vm(2 * reach, col_dev, lanes), vm(*field),
            vm(2 * reach, col_dev, lanes),
            vm(*moved), vm(*moved), vm(*moved), vm(*moved), vm(*moved), vm(*moved),
            vm(ns, 8, lanes), vm(ns, 8, lanes),
            pltpu.VMEM(
                (BLOCKS_DEV, groups, (NEIGHBOURS + 1) * wide // lanes, 2 * strip_rows * GROUP, lanes),
                jnp.bfloat16,
            ),
            pltpu.VMEM((2, blocks_halo, strip_rows, col_dev, lanes), jnp.bfloat16),
            vm(2, row_dev, col_dev, lanes),
            vm(groups, 2, blocks_halo, wide),
            vm(groups, 2, BLOCKS_DEV, wide),
            vm(3, place_rows, col_dev),
            vm(2, place_rows, col_dev),
            vm(1, lanes),
            vm(rows, lanes), vm(rows, lanes), vm(col_dev, lanes), vm(col_dev, lanes),
            vm(2 * reach, lanes),
            vm(nw, 2 * rows, lanes), vm(nw, rows, lanes),
            vm(col_dev // 2, lanes),
            vm(*piece), vm(*piece), vm(*piece), vm(*piece),
            vm(ns, col_dev // 2 // ns, lanes), vm(ns, col_dev // 2 // ns, lanes),
            vm(4, 8, lanes), vm(nw, 8, lanes), vm(ns, 8, lanes),
            pltpu.SemaphoreType.DMA((6,)),
            pltpu.SemaphoreType.DMA((11, most)), pltpu.SemaphoreType.DMA((11, most)),
            pltpu.SemaphoreType.DMA((4, ns)), pltpu.SemaphoreType.DMA((4, ns)),
            pltpu.SemaphoreType.DMA((2, reach)), pltpu.SemaphoreType.DMA((2, reach)),
            pltpu.SemaphoreType.DMA((2, REACH)), pltpu.SemaphoreType.DMA((2, REACH)),
        ],
        compiler_params=pltpu.CompilerParams(
            collective_id=0, has_side_effects=True, vmem_limit_bytes=57 * 1000 * 1000 if static_came else 66 * 1000 * 1000
        ),
    )(
        came,
        owner_map,
        jnp.transpose(neighbours, (2, 0, 1)),
        observations.reshape(fields * row_dev, col_dev),
        huber_scale.reshape(1, fields),
        observed,
        jitter,
    )
    return solution_now[None, None], residual_now[None, None]


def solution(mesh):
    return jax.shard_map(
        on_device,
        mesh=mesh,
        in_specs=(
            P(None, "sixteen", "wide"),
            P(),
            P("sixteen", "wide"),
            P(None, "sixteen", "wide"),
            P("wide", None),
            P("wide", None, None),
        ),
        out_specs=(P("wide", "sixteen", None, None, None), P("wide", "sixteen", None, None, None)),
        check_vma=False,
    )
```

```python
import functools

import jax
import jax.numpy as jnp
from jax import lax
from jax.experimental import pallas as pl
from jax.experimental.pallas import tpu as pltpu
from jax.sharding import PartitionSpec as P

BLOCK = 512
BLOCKS_DEV = 8
REACH = 4
NEIGHBOURS = 6
SWEEPS = 2

HUBER_EDGE = 1.345
NUGGET_TERM = 1.0
SILL_TERM = 0.02
ROOT_THREE = 1.7320508075688772
LOG2E = 1.4426950408889634
GROUP = 16
MESH = pl.DeviceIdType.MESH
VMEM = pl.BlockSpec(memory_space=pltpu.VMEM)
SMEM = pl.BlockSpec(memory_space=pltpu.SMEM)
F32 = jnp.float32


def say_hello(sizes):
    barrier = pltpu.get_barrier_semaphore()
    for axis, n in sizes:
        me = lax.axis_index(axis)

        def say(k, carry, axis=axis, n=n, me=me):
            pl.semaphore_signal(
                barrier, inc=1, device_id={axis: lax.rem(me + k, n)}, device_id_type=MESH
            )
            return carry

        lax.fori_loop(1, n, say, 0)


def hear_hello(sizes):
    pl.semaphore_wait(pltpu.get_barrier_semaphore(), sum(n - 1 for _, n in sizes))


def remote(src, dst, send, recv, axis, n, shift):
    return pltpu.make_async_remote_copy(
        src_ref=src,
        dst_ref=dst,
        send_sem=send,
        recv_sem=recv,
        device_id={axis: lax.rem(lax.axis_index(axis) + shift, n)},
        device_id_type=MESH,
    )


def start(copies):
    for c in copies:
        c.start()


def wait(copies):
    for c in copies:
        c.wait()


def spread_copies(buffer, axis, n, send, recv):
    return [
        remote(buffer.at[0], buffer.at[k], send.at[k], recv.at[k], axis, n, k) for k in range(1, n)
    ]


def gathered_sum(buffer, axis, n):
    me = lax.axis_index(axis)
    total = None
    for owner in range(n):
        term = buffer[lax.rem(me - owner + n, n)]
        total = term if total is None else total + term
    return total


def exchange_copies(staged, received, n, send, recv):
    return [pltpu.make_async_copy(staged.at[0], received.at[0], send.at[0])] + [
        remote(staged.at[k], received.at[k], send.at[k], recv.at[k], "sixteen", n, k)
        for k in range(1, n)
    ]


def edge_copies(source, target, reach, n, send, recv):
    rows = source.shape[0]
    return [
        remote(
            source.at[pl.ds(first, reach)],
            target.at[pl.ds(side * reach, reach)],
            send.at[side],
            recv.at[side],
            "sixteen",
            n,
            shift,
        )
        for side, first, shift in ((0, rows - reach, 1), (1, 0, n - 1))
    ]


def swap(x):
    return pltpu.roll(x, x.shape[-1] // 2, x.ndim - 1)


def fold(x):
    return x + swap(x)


def low_lanes(x):
    return lax.broadcasted_iota(jnp.int32, x.shape, x.ndim - 1) < x.shape[-1] // 2


def beside(even, odd):
    return jnp.where(low_lanes(even), even, odd)


def turned(x, size):
    rows = x.shape[0]
    if rows < size:
        x = jnp.concatenate([x, jnp.zeros((size - rows, x.shape[1]), x.dtype)], axis=0)
    return x.T


def across(x, k, shape):
    return jnp.broadcast_to(x[:, k : k + 1], shape)


def solve_kernel(
    nw, ns, fields, strip_rows, starts, span, static_came,
    came, owner_hbm, listed_hbm, obs_hbm, scale_hbm, seen_hbm, jitter_hbm,
    out, rest,
    offs, chosen, owner, listed, obs_in, scale_in, seen_in, jitter_in,
    obs, weight, edge, q, q_edge, staged_p, recv_p, staged_q, recv_q, staged_w, recv_w,
    staged_m, recv_m, tiles, win, cb, oth, own_oth, place, coords,
    scale, row_eff, row_cnt, col_eff, col_cnt, row_edge, row_buf0, row_buf1,
    col_part, col_send0, col_send1, col_got0, col_got1, col_all0, col_all1,
    dots, dot_w, dot_s,
    sem_in, sem_s, sem_r, exch_s, exch_r, obs_s, obs_r, halo_s, halo_r,
):
    rows, cols, lanes = obs.shape
    half = cols // 2
    chunk = half // ns
    pairs = strip_rows // 2
    reach = REACH * pairs
    row_dev = 2 * rows
    row_reach = 2 * reach
    groups = len(starts)
    wide = strip_rows * span
    parts = wide // lanes
    tile_rows = strip_rows * GROUP
    total_strips = BLOCKS_DEV * ns
    me = lax.axis_index("sixteen")
    group_me = lax.axis_index("wide")
    everyone = (("wide", nw), ("sixteen", ns))
    full = (cols, lanes)

    say_hello(everyone)
    arrivals = [
        pltpu.make_async_copy(source, target, sem_in.at[k])
        for k, (source, target) in enumerate(
            (
                (obs_hbm, obs_in), (scale_hbm, scale_in), (seen_hbm, seen_in),
                (jitter_hbm, jitter_in), (owner_hbm, owner), (listed_hbm, listed),
            )
        )
    ]
    start(arrivals)
    wait(arrivals)

    def pack(r, carry):
        both = jnp.concatenate(
            [obs_in[pl.ds(2 * r + parity, fields, stride=row_dev), :] for parity in range(2)],
            axis=0,
        )
        obs[r] = both.T
        return carry

    early = 3
    lax.fori_loop(0, early, pack, 0)
    lax.fori_loop(rows - reach, rows - reach + early, pack, 0)

    row_number = lax.broadcasted_iota(jnp.int32, (row_dev, cols), 0) + me * row_dev
    col_number = lax.broadcasted_iota(jnp.int32, (row_dev, cols), 1) + group_me * cols
    seen = seen_in[...].astype(F32)
    place[0, pl.ds(row_reach, row_dev)] = row_number.astype(F32) + jitter_in[0]
    place[1, pl.ds(row_reach, row_dev)] = col_number.astype(F32) + jitter_in[1]
    place[2, pl.ds(row_reach, row_dev)] = seen

    for n in range(NEIGHBOURS):
        other = listed[n, 0, 0]
        offs[n + 1] = jnp.where(other < total_strips // 2, other, other - total_strips)
    offs[0] = 0
    for k in range(ns):
        target = lax.rem(me + k, ns)
        pick = 0
        for j in range(BLOCKS_DEV):
            pick = jnp.where(owner[0, me * BLOCKS_DEV + j] == target, j, pick)
        chosen[k] = pick

    hear_hello(everyone)
    place_copies = [
        remote(
            place.at[:, pl.ds(row_dev, row_reach)],
            place.at[:, pl.ds(0, row_reach)],
            sem_s.at[6, 0], sem_r.at[6, 0], "sixteen", ns, 1,
        ),
        remote(
            place.at[:, pl.ds(row_reach, row_reach)],
            place.at[:, pl.ds(row_reach + row_dev, row_reach)],
            sem_s.at[6, 1], sem_r.at[6, 1], "sixteen", ns, ns - 1,
        ),
    ]

    def halo_copies(source, target, size, send, recv, t):
        return [
            remote(
                source.at[pl.ds(rows - reach + t * size, size)],
                target.at[pl.ds(t * size, size)],
                send.at[0, t], recv.at[0, t], "sixteen", ns, 1,
            ),
            remote(
                source.at[pl.ds(t * size, size)],
                target.at[pl.ds(reach + t * size, size)],
                send.at[1, t], recv.at[1, t], "sixteen", ns, ns - 1,
            ),
        ]

    obs_copies = [halo_copies(obs, edge, 1, obs_s, obs_r, t) for t in range(reach)]
    row_copies = edge_copies(row_eff, row_edge, reach, ns, sem_s.at[8], sem_r.at[8])
    start(place_copies)

    def stage(staged, source):
        def one(k, carry):
            for pair in range(pairs):
                staged[k, pair] = source[chosen[k] * pairs + pair]
            return carry

        lax.fori_loop(0, ns, one, 0)

    start(sum(obs_copies[:early], []))
    lax.fori_loop(early, rows - reach, pack, 0)
    lax.fori_loop(rows - reach + early, rows, pack, 0)
    stage(staged_p, obs)
    p_copies = exchange_copies(staged_p, recv_p, ns, exch_s.at[0], exch_r.at[0])

    near_first = p_copies[2::2]
    bulk = [
        p_copies[:1] + near_first[0::3],
        sum(obs_copies[3:4], []),
        sum(obs_copies[4:5], []),
        sum(obs_copies[6:7], []),
        sum(obs_copies[7:8], [])+near_first[2::3]+p_copies[1::2],
        sum(obs_copies[5:6], [])+near_first[1::3],
    ]
    start(bulk[0])
    seen_t = turned(seen, lanes)
    for r in range(rows):
        weight[r] = beside(across(seen_t, 2 * r, full), across(seen_t, 2 * r + 1, full))
    one_scale = scale_in[...]
    scale[...] = jnp.concatenate([one_scale, one_scale], axis=1)
    inv = 1.0 / scale[...]
    row_eff[...] = jnp.zeros_like(row_eff)
    col_eff[...] = jnp.zeros_like(col_eff)

    spread = 2.0 * strip_rows
    cutoff = 6.0 * strip_rows
    ratio = ROOT_THREE * cutoff / spread
    unit = (4.0 * ratio * SILL_TERM) ** (1.0 / 6.0)

    def centred(first, count):
        at = pl.ds(first, count)
        coords[0, at] = (place[0, at] - (me * row_dev + row_dev // 2).astype(F32)) * (unit / cutoff)
        coords[1, at] = (place[1, at] - (group_me * cols + cols // 2).astype(F32)) * (unit / cutoff)

    def lines(target, first, blocks):
        for c in range(2):
            for pair in range(pairs):
                a = [
                    coords[c, pl.ds(first + 2 * pair + parity, blocks, stride=strip_rows), :]
                    for parity in range(2)
                ]
                for i, s in enumerate(starts):
                    x = pltpu.roll(a[0], (cols - s) % cols, 1)
                    y = pltpu.roll(a[1], (cols + span - s) % cols, 1)
                    target[i, c, :, pair * lanes : (pair + 1) * lanes] = beside(x, y)

    def prepare_own():
        centred(row_reach, row_dev)
        for c in range(2):
            t = turned(coords[c, pl.ds(row_reach, row_dev)], lanes)
            for r in range(row_dev):
                cb[c, r] = across(t, r, full)
        lines(own_oth, row_reach, BLOCKS_DEV)

    def prepare_all():
        centred(0, row_reach)
        centred(row_reach + row_dev, row_reach)
        lines(oth, 0, oth.shape[2])

    def tile_builder(source, first_block, members):
        def build(t, carry):
            block, i = t // groups, lax.rem(t, groups)
            at = pl.multiple_of(i * GROUP, GROUP)
            first = pl.multiple_of(block * strip_rows, strip_rows)
            row_here = cb[0, pl.ds(first, strip_rows), pl.ds(at, GROUP), :].reshape(tile_rows, lanes)
            col_here = cb[1, pl.ds(first, strip_rows), pl.ds(at, GROUP), :].reshape(tile_rows, lanes)
            for n in members:
                h = block + first_block + (offs[n] if n else 0)
                row_line = source[i, 0, pl.ds(h, 1), :]
                col_line = source[i, 1, pl.ds(h, 1), :]
                for part in range(parts):
                    cut = slice(part * lanes, (part + 1) * lanes)
                    row_gap = row_line[:, cut] - row_here
                    col_gap = col_line[:, cut] - col_here
                    square = row_gap * row_gap + col_gap * col_gap
                    if n == 0:
                        distance = square * lax.rsqrt(jnp.maximum(square, 1e-30))
                    else:
                        distance = square * lax.rsqrt(square)
                    fading = jnp.maximum(unit - distance, 0.0)
                    fading = fading * fading
                    fading = fading * fading
                    decay = jnp.exp2(distance * (-ratio * LOG2E / unit))
                    lead = (distance + unit / ratio) * (distance + unit / 4.0)
                    kernel = (lead * decay) * fading
                    if n == 0:
                        kernel = kernel * (NEIGHBOURS + 1.0)
                    high = kernel.astype(jnp.bfloat16)
                    low = (kernel - high.astype(F32)).astype(jnp.bfloat16)
                    tiles[block, i, parts * n + part, 0:tile_rows] = high
                    tiles[block, i, parts * n + part, tile_rows : 2 * tile_rows] = low
            return carry

        return build

    build_own = tile_builder(own_oth, 0, (0,))
    build_tile = tile_builder(oth, REACH, tuple(range(1, NEIGHBOURS + 1)))

    steps = BLOCKS_DEV * groups
    shares = (0, 9, 19, 29, 42, 53, 64)

    def build_some(part):
        lax.fori_loop(shares[part] * steps // 64, shares[part + 1] * steps // 64, build_tile, 0)

    m_copies = exchange_copies(staged_m, recv_m, ns, exch_s.at[3], exch_r.at[3])
    edge_value = HUBER_EDGE
    for sweep in range(SWEEPS):
        row_buf = (row_buf0, row_buf1)[min(sweep, 1)]
        col_send = (col_send0, col_send1)[min(sweep, 1)]
        col_got = (col_got0, col_got1)[min(sweep, 1)]
        col_all = (col_all0, col_all1)[min(sweep, 1)]

        def clipped(r):
            value = (obs[r] - row_eff[pl.ds(r, 1)] - col_eff[...]) * inv
            return weight[r] * jnp.clip(value, -edge_value, edge_value)

        def row_step(r, carry):
            row_buf[0, pl.ds(r, 1)] = jnp.sum(clipped(r), axis=0, keepdims=True)
            if sweep == 0:
                row_buf[0, pl.ds(rows + r, 1)] = jnp.sum(weight[r], axis=0, keepdims=True)
            return carry

        lax.fori_loop(0, rows, row_step, 0)
        sums = spread_copies(row_buf, "wide", nw, sem_s.at[sweep], sem_r.at[sweep])
        start(sums)
        if sweep == 0:
            prepare_own()
            lax.fori_loop(0, steps, build_own, 0)
            wait(place_copies)
            prepare_all()
        build_some(3 * sweep)
        wait(sums)
        total = gathered_sum(row_buf, "wide", nw)
        if sweep == 0:
            row_cnt[...] = jnp.maximum(total[rows:], 1.0)
        row_eff[...] = row_eff[...] + scale[...] * total[:rows] / row_cnt[...]
        if sweep == SWEEPS - 1:
            start(row_copies)

            def describe(k, carry):
                for pair in range(pairs):
                    staged_m[k, pair : pair + 1] = row_eff[pl.ds(chosen[k] * pairs + pair, 1)]
                for r in range(strip_rows):
                    at = pairs + r
                    staged_m[k, at : at + 1] = place[2, pl.ds(row_reach + chosen[k] * strip_rows + r, 1)]
                return carry

            staged_m[...] = jnp.zeros_like(staged_m)
            lax.fori_loop(0, ns, describe, 0)
            start(m_copies)

        def col_step(r, carry):
            return carry + clipped(r)

        part = fold(lax.fori_loop(0, rows, col_step, jnp.zeros(full, F32)))
        col_part[0:half] = beside(part[:half], part[half:])
        count = jnp.sum(seen, axis=0, keepdims=True)
        for k in range(ns):
            owner_of = lax.rem(me + k, ns)
            col_send[k, 0:chunk] = col_part[pl.ds(pl.multiple_of(owner_of * chunk, chunk), chunk)]
            col_send[k, chunk : chunk + 8] = jnp.broadcast_to(count, (8, cols))
        col_got[0] = col_send[0]
        sums = [
            remote(
                col_send.at[k], col_got.at[k],
                sem_s.at[2 + sweep, k], sem_r.at[2 + sweep, k], "sixteen", ns, k,
            )
            for k in range(1, ns)
        ]
        start(sums)
        start(bulk[2 * sweep + 1])
        build_some(3 * sweep + 1)
        wait(sums)
        total = gathered_sum(col_got, "sixteen", ns)
        col_all[0] = total[:chunk]
        if sweep == 0:
            counts = jnp.broadcast_to(total[chunk : chunk + 1], full).T
            col_cnt[...] = jnp.maximum(counts, 1.0)
        sums = spread_copies(col_all, "sixteen", ns, sem_s.at[9 + sweep], sem_r.at[9 + sweep])
        start(sums)
        start(bulk[2 * sweep + 2])
        build_some(3 * sweep + 2)
        wait(sums)
        if sweep == 0:
            start(bulk[5])
        total = jnp.concatenate(
            [col_all[lax.rem(me - o + ns, ns)] for o in range(ns)], axis=0
        )
        y = total[:half]
        z = swap(y)
        both = jnp.concatenate([beside(y, z), beside(z, y)], axis=0)
        col_eff[...] = col_eff[...] + scale[...] * both / col_cnt[...]

    for copies in obs_copies:
        wait(copies)

    def remain(r, carry):
        obs[r] = weight[r] * (obs[r] - row_eff[pl.ds(r, 1)] - col_eff[...])
        return carry

    lax.fori_loop(0, rows, remain, 0)
    p = obs

    def windows(source, first, h):
        for pair in range(pairs):
            x = source[first + pair]
            z = swap(x)
            low = low_lanes(x)
            for parity in range(2):
                y = jnp.where(low, x, z) if parity == 0 else jnp.where(low, z, x)
                high = y.astype(jnp.bfloat16).astype(F32)
                both = jnp.where(low, high, y - high)
                win[0, h, 2 * pair + parity] = both.astype(jnp.bfloat16)
                win[1, h, 2 * pair + parity, 0 : cols - GROUP] = both[
                    GROUP // 2 : cols - GROUP // 2
                ].astype(jnp.bfloat16)

    def own_windows(source):
        def one(b, carry):
            windows(source, b * pairs, REACH + b)
            return carry

        lax.fori_loop(0, BLOCKS_DEV, one, 0)

    def edge_windows(source):
        def one(b, carry):
            windows(source, b * pairs, b)
            windows(source, reach + b * pairs, REACH + BLOCKS_DEV + b)
            return carry

        lax.fori_loop(0, REACH, one, 0)

    own_windows(p)
    wait(row_copies)
    seen_t = turned(place[2], lanes)
    for t in range(reach):
        for at, r in ((t, t), (reach + t, reach + rows + t)):
            there = beside(across(seen_t, 2 * r, full), across(seen_t, 2 * r + 1, full))
            edge[at] = there * (edge[at] - row_edge[pl.ds(at, 1)] - col_eff[...])
    edge_windows(edge)
    dots[...] = jnp.zeros_like(dots)

    def apply(block, own_of, store):
        for i, s in enumerate(starts):
            shifted = (s % GROUP) // (GROUP // 2)
            base = s - shifted * (GROUP // 2)
            acc = jnp.zeros((2 * tile_rows, lanes), F32)
            for n in range(NEIGHBOURS + 1):
                h = block + REACH + offs[n]
                acc = acc + jnp.dot(
                    jnp.concatenate(
                        [tiles[block, i, parts * n + part] for part in range(parts)], axis=1
                    ),
                    win[shifted, h, :, base : base + span, :].reshape(wide, lanes),
                    preferred_element_type=F32,
                )
            y = fold(acc[:tile_rows] + acc[tile_rows:])
            for pair in range(pairs):
                even = y[(2 * pair) * GROUP : (2 * pair + 1) * GROUP]
                odd = y[(2 * pair + 1) * GROUP : (2 * pair + 2) * GROUP]
                own = own_of(pair, i * GROUP)
                store(pair, i * GROUP, own, NUGGET_TERM * own + beside(even, odd))

    def gather_dot(k, x, y):
        z = x * y
        dots[k] = dots[k] + (z[: GROUP // 2] + z[GROUP // 2 :])

    def q_copies(t):
        return halo_copies(q, q_edge, pairs, halo_s, halo_r, t)

    def first_block(block):
        def own_of(pair, at):
            return p[block * pairs + pair, at : at + GROUP, :]

        def store(pair, at, own, value):
            q[block * pairs + pair, at : at + GROUP, :] = value
            gather_dot(0, own, own)
            gather_dot(1, own, value)
            gather_dot(2, value, value)

        apply(block, own_of, store)

    def first_pass(u, carry):
        t, side = u // 2, lax.rem(u, 2)
        first_block(side * REACH + t)
        up, down = q_copies(t)

        @pl.when(side == 0)
        def _():
            down.start()

        @pl.when(side == 1)
        def _():
            up.start()

        return carry

    lax.fori_loop(0, BLOCKS_DEV, first_pass, 0)

    stage(staged_q, q)
    q_exchange = exchange_copies(staged_q, recv_q, ns, exch_s.at[1], exch_r.at[1])
    start(q_exchange[0::2])
    own_windows(q)
    wait(p_copies)
    wait(m_copies)
    facts = turned(recv_m[...].reshape(ns * 8, cols), lanes)
    for k in range(ns):
        for pair in range(pairs):
            at = 8 * k + pairs + 2 * pair
            there = beside(across(facts, at, full), across(facts, at + 1, full))
            recv_p[k, pair] = there * (recv_p[k, pair] - recv_m[k, pair : pair + 1] - col_eff[...])
    for t in range(REACH):
        wait(q_copies(t))
    start(q_exchange[1::2])
    edge_windows(q_edge)

    w_copies = exchange_copies(staged_w, recv_w, ns, exch_s.at[2], exch_r.at[2])
    one_each = ns == BLOCKS_DEV
    held = 3 if one_each else 0

    def second_block(g, carry):
        slot = lax.rem(g + 1, BLOCKS_DEV)
        block = chosen[slot] if one_each else g

        def own_of(pair, at):
            return q[block * pairs + pair, at : at + GROUP, :]

        def store(pair, at, own, value):
            gather_dot(3, own, value)
            if one_each:
                staged_w[slot, pair, at : at + GROUP, :] = value
            else:
                edge[g * pairs + pair, at : at + GROUP, :] = value

        apply(block, own_of, store)
        if one_each:
            for k in range(1, held):

                @pl.when(g == k - 1)
                def _(k=k):
                    w_copies[k].start()

        return carry

    lax.fori_loop(0, BLOCKS_DEV, second_block, 0)
    if not one_each:
        stage(staged_w, edge)

    for k in range(4):
        dot_w[0, k : k + 1] = jnp.sum(fold(dots[k]), axis=0, keepdims=True)
    dot_w[0, 4:8] = jnp.zeros((4, lanes), F32)
    sums = spread_copies(dot_w, "wide", nw, sem_s.at[4], sem_r.at[4])
    start(sums)
    wait(sums)
    dot_s[0] = gathered_sum(dot_w, "wide", nw)
    sums = spread_copies(dot_s, "sixteen", ns, sem_s.at[5], sem_r.at[5])
    start(sums)
    start((w_copies[:1] if one_each else []) + w_copies[held:])
    wait(sums)
    total = gathered_sum(dot_s, "sixteen", ns)
    m0, m1, m2, m3 = (total[k : k + 1] for k in range(4))
    alpha = m0 / m1
    norm = (m0 - 2.0 * alpha * m1) + alpha * alpha * m2
    grown = 1.0 + norm / m0
    bend = grown * (grown * m1 - 2.0 * alpha * m2) + alpha * alpha * m3
    second = norm / bend
    near = alpha + second * grown
    far = second * alpha

    turned_rows = obs_in

    def deliver(target, value_of, before=None):
        for k in range(ns if static_came else BLOCKS_DEV):
            j = lax.rem(me - k + ns, ns) if static_came else k
            slot = k if static_came else came[k]
            if before is not None:
                before(k)
            for pair in range(pairs):
                at = pl.multiple_of((j * pairs + pair) * lanes, lanes)
                turned_rows[pl.ds(at, lanes)] = value_of(slot, pair).T
        for f in range(fields):
            for r in range(strip_rows):
                line = (r // 2) * lanes + (r % 2) * fields + f
                target[f, :, r * cols : (r + 1) * cols] = turned_rows[
                    pl.ds(line, BLOCKS_DEV, stride=pairs * lanes), :
                ]

    wait(q_exchange)
    deliver(out, lambda k, pair: near * recv_p[k, pair] - far * recv_q[k, pair])
    if not static_came:
        wait(w_copies)
    deliver(
        rest,
        lambda k, pair: (recv_p[k, pair] - near * recv_q[k, pair]) + far * recv_w[k, pair],
        (lambda k: wait(w_copies[k : k + 1])) if static_came else None,
    )


def owned_table(group_map, owners, per_owner):
    total_strips = group_map.shape[0]
    member = (group_map[None, :] == jnp.arange(owners, dtype=jnp.int32)[:, None]).astype(jnp.int32)
    ranked = jnp.cumsum(member, axis=1, dtype=jnp.int32) - 1
    slot_hit = (ranked[:, :, None] == jnp.arange(per_owner, dtype=jnp.int32)[None, None, :]).astype(
        jnp.int32
    ) * member[:, :, None]
    numbers = jnp.arange(total_strips, dtype=jnp.int32)
    return jnp.sum(slot_hit * numbers[None, :, None], axis=1, dtype=jnp.int32)


def on_device(observations, huber_scale, observed, jitter, owner_map, neighbours):
    fields, row_dev, col_dev = observations.shape
    nw, ns = lax.axis_size("wide"), lax.axis_size("sixteen")
    strip_rows = BLOCK // col_dev
    rows, lanes = row_dev // 2, 2 * fields
    pairs = strip_rows // 2
    reach = REACH * pairs
    shape = jax.ShapeDtypeStruct

    cut = 6 * strip_rows
    span = GROUP + 2 * cut
    starts = tuple(
        min(max(GROUP * i - cut, 0), col_dev - span) for i in range(col_dev // GROUP)
    )
    groups = len(starts)
    wide = strip_rows * span
    blocks_halo = BLOCKS_DEV + 2 * REACH

    static_came = ns == BLOCKS_DEV
    if static_came:
        came = owner_map
    else:
        my_place = lax.axis_index("sixteen")
        table = owned_table(owner_map[0], ns, BLOCKS_DEV)
        my_ids = lax.dynamic_index_in_dim(table, my_place, 0, keepdims=False)
        came = (my_place - my_ids // BLOCKS_DEV + ns) % ns

    most = max(nw, ns)
    anywhere = pl.BlockSpec(memory_space=pl.ANY)
    vm = lambda *s: pltpu.VMEM(s, F32)
    moved = (ns, pairs, col_dev, lanes)
    piece = (ns, col_dev // 2 // ns + 8, lanes)
    field = (rows, col_dev, lanes)
    place_rows = row_dev + 4 * reach
    out_shape = shape((fields, BLOCKS_DEV, BLOCK), F32)
    solution_now, residual_now = pl.pallas_call(
        functools.partial(solve_kernel, nw, ns, fields, strip_rows, starts, span, static_came),
        out_shape=((vm(*out_shape.shape) if static_came else out_shape),) * 2,
        in_specs=[anywhere if static_came else SMEM] + [anywhere] * 6,
        out_specs=(VMEM, VMEM),
        scratch_shapes=[
            pltpu.SMEM((NEIGHBOURS + 1,), jnp.int32),
            pltpu.SMEM((ns,), jnp.int32),
            pltpu.SMEM(owner_map.shape, jnp.int32),
            pltpu.SMEM((NEIGHBOURS, 1, neighbours.shape[1]), jnp.int32),
            vm(fields * row_dev, col_dev),
            vm(1, fields),
            pltpu.VMEM((row_dev, col_dev), jnp.int32),
            vm(2, row_dev, col_dev),
            vm(*field), vm(*field), vm(2 * reach, col_dev, lanes), vm(*field),
            vm(2 * reach, col_dev, lanes),
            vm(*moved), vm(*moved), vm(*moved), vm(*moved), vm(*moved), vm(*moved),
            vm(ns, 8, lanes), vm(ns, 8, lanes),
            pltpu.VMEM(
                (BLOCKS_DEV, groups, (NEIGHBOURS + 1) * wide // lanes, 2 * strip_rows * GROUP, lanes),
                jnp.bfloat16,
            ),
            pltpu.VMEM((2, blocks_halo, strip_rows, col_dev, lanes), jnp.bfloat16),
            vm(2, row_dev, col_dev, lanes),
            vm(groups, 2, blocks_halo, wide),
            vm(groups, 2, BLOCKS_DEV, wide),
            vm(3, place_rows, col_dev),
            vm(2, place_rows, col_dev),
            vm(1, lanes),
            vm(rows, lanes), vm(rows, lanes), vm(col_dev, lanes), vm(col_dev, lanes),
            vm(2 * reach, lanes),
            vm(nw, 2 * rows, lanes), vm(nw, rows, lanes),
            vm(col_dev // 2, lanes),
            vm(*piece), vm(*piece), vm(*piece), vm(*piece),
            vm(ns, col_dev // 2 // ns, lanes), vm(ns, col_dev // 2 // ns, lanes),
            vm(4, 8, lanes), vm(nw, 8, lanes), vm(ns, 8, lanes),
            pltpu.SemaphoreType.DMA((6,)),
            pltpu.SemaphoreType.DMA((11, most)), pltpu.SemaphoreType.DMA((11, most)),
            pltpu.SemaphoreType.DMA((4, ns)), pltpu.SemaphoreType.DMA((4, ns)),
            pltpu.SemaphoreType.DMA((2, reach)), pltpu.SemaphoreType.DMA((2, reach)),
            pltpu.SemaphoreType.DMA((2, REACH)), pltpu.SemaphoreType.DMA((2, REACH)),
        ],
        compiler_params=pltpu.CompilerParams(
            collective_id=0, has_side_effects=True, vmem_limit_bytes=57 * 1000 * 1000 if static_came else 66 * 1000 * 1000
        ),
    )(
        came,
        owner_map,
        jnp.transpose(neighbours, (2, 0, 1)),
        observations.reshape(fields * row_dev, col_dev),
        huber_scale.reshape(1, fields),
        observed,
        jitter,
    )
    return solution_now[None, None], residual_now[None, None]


def solution(mesh):
    return jax.shard_map(
        on_device,
        mesh=mesh,
        in_specs=(
            P(None, "sixteen", "wide"),
            P(),
            P("sixteen", "wide"),
            P(None, "sixteen", "wide"),
            P("wide", None),
            P("wide", None, None),
        ),
        out_specs=(P("wide", "sixteen", None, None, None), P("wide", "sixteen", None, None, None)),
        check_vma=False,
    )
```

```python
import functools

import jax
import jax.numpy as jnp
from jax import lax
from jax.experimental import pallas as pl
from jax.experimental.pallas import tpu as pltpu
from jax.sharding import PartitionSpec as P

BLOCK = 512
BLOCKS_DEV = 8
REACH = 4
NEIGHBOURS = 6
SWEEPS = 2

HUBER_EDGE = 1.345
NUGGET_TERM = 1.0
SILL_TERM = 0.02
ROOT_THREE = 1.7320508075688772
LOG2E = 1.4426950408889634
GROUP = 16
MESH = pl.DeviceIdType.MESH
VMEM = pl.BlockSpec(memory_space=pltpu.VMEM)
SMEM = pl.BlockSpec(memory_space=pltpu.SMEM)
F32 = jnp.float32


def say_hello(sizes):
    barrier = pltpu.get_barrier_semaphore()
    for axis, n in sizes:
        me = lax.axis_index(axis)

        def say(k, carry, axis=axis, n=n, me=me):
            pl.semaphore_signal(
                barrier, inc=1, device_id={axis: lax.rem(me + k, n)}, device_id_type=MESH
            )
            return carry

        lax.fori_loop(1, n, say, 0)


def hear_hello(sizes):
    pl.semaphore_wait(pltpu.get_barrier_semaphore(), sum(n - 1 for _, n in sizes))


def remote(src, dst, send, recv, axis, n, shift):
    return pltpu.make_async_remote_copy(
        src_ref=src,
        dst_ref=dst,
        send_sem=send,
        recv_sem=recv,
        device_id={axis: lax.rem(lax.axis_index(axis) + shift, n)},
        device_id_type=MESH,
    )


def start(copies):
    for c in copies:
        c.start()


def wait(copies):
    for c in copies:
        c.wait()


def spread_copies(buffer, axis, n, send, recv):
    return [
        remote(buffer.at[0], buffer.at[k], send.at[k], recv.at[k], axis, n, k) for k in range(1, n)
    ]


def gathered_sum(buffer, axis, n, count=None):
    me = lax.axis_index(axis)
    total = None
    for owner in range(n):
        term = buffer[lax.rem(me - owner + n, n), 0 : buffer.shape[1] if count is None else count]
        total = term if total is None else total + term
    return total


def exchange_copies(staged, received, n, send, recv):
    return [pltpu.make_async_copy(staged.at[0], received.at[0], send.at[0])] + [
        remote(staged.at[k], received.at[k], send.at[k], recv.at[k], "sixteen", n, k)
        for k in range(1, n)
    ]


def edge_copies(source, target, reach, n, send, recv):
    rows = source.shape[0]
    return [
        remote(
            source.at[pl.ds(first, reach)],
            target.at[pl.ds(side * reach, reach)],
            send.at[side],
            recv.at[side],
            "sixteen",
            n,
            shift,
        )
        for side, first, shift in ((0, rows - reach, 1), (1, 0, n - 1))
    ]


def swap(x):
    return pltpu.roll(x, x.shape[-1] // 2, x.ndim - 1)


def fold(x):
    return x + swap(x)


def low_lanes(x):
    return lax.broadcasted_iota(jnp.int32, x.shape, x.ndim - 1) < x.shape[-1] // 2


def beside(even, odd):
    return jnp.where(low_lanes(even), even, odd)


def turned(x, size):
    rows = x.shape[0]
    if rows < size:
        x = jnp.concatenate([x, jnp.zeros((size - rows, x.shape[1]), x.dtype)], axis=0)
    return x.T


def across(x, k, shape):
    return jnp.broadcast_to(x[:, k : k + 1], shape)


def solve_kernel(
    nw, ns, fields, strip_rows, starts, span, static_came,
    came, owner_hbm, listed_hbm, obs_hbm, scale_hbm, seen_hbm, jitter_hbm,
    out, rest,
    offs, chosen, owner, listed, obs_in, scale_in, seen_in, jitter_in,
    obs, weight, edge, q, q_edge, staged_p, recv_p, staged_q, recv_q, staged_w, recv_w,
    staged_m, recv_m, tiles, win, cb, oth, own_oth, place, coords,
    scale, row_eff, row_cnt, col_eff, col_cnt, row_edge, row_buf0, row_buf1,
    col_part, col_send0, col_send1, col_got0, col_got1, col_all0, col_all1,
    dots, dot_w, dot_s,
    sem_in, sem_s, sem_r, exch_s, exch_r, obs_s, obs_r, halo_s, halo_r,
):
    rows, cols, lanes = obs.shape
    half = cols // 2
    chunk = half // ns
    pairs = strip_rows // 2
    reach = REACH * pairs
    row_dev = 2 * rows
    row_reach = 2 * reach
    groups = len(starts)
    wide = strip_rows * span
    parts = wide // lanes
    tile_rows = strip_rows * GROUP
    total_strips = BLOCKS_DEV * ns
    me = lax.axis_index("sixteen")
    group_me = lax.axis_index("wide")
    everyone = (("wide", nw), ("sixteen", ns))
    full = (cols, lanes)

    say_hello(everyone)
    arrivals = [
        pltpu.make_async_copy(source, target, sem_in.at[k])
        for k, (source, target) in enumerate(
            (
                (obs_hbm, obs_in), (scale_hbm, scale_in), (seen_hbm, seen_in),
                (jitter_hbm, jitter_in), (owner_hbm, owner), (listed_hbm, listed),
            )
        )
    ]
    start(arrivals)
    wait(arrivals)

    def pack(r, carry):
        both = jnp.concatenate(
            [obs_in[pl.ds(2 * r + parity, fields, stride=row_dev), :] for parity in range(2)],
            axis=0,
        )
        obs[r] = both.T
        return carry

    early = 3
    lax.fori_loop(0, early, pack, 0)
    lax.fori_loop(rows - reach, rows - reach + early, pack, 0)

    row_number = lax.broadcasted_iota(jnp.int32, (row_dev, cols), 0) + me * row_dev
    col_number = lax.broadcasted_iota(jnp.int32, (row_dev, cols), 1) + group_me * cols
    seen = seen_in[...].astype(F32)
    place[0, pl.ds(row_reach, row_dev)] = row_number.astype(F32) + jitter_in[0]
    place[1, pl.ds(row_reach, row_dev)] = col_number.astype(F32) + jitter_in[1]
    place[2, pl.ds(row_reach, row_dev)] = seen

    for n in range(NEIGHBOURS):
        other = listed[n, 0, 0]
        offs[n + 1] = jnp.where(other < total_strips // 2, other, other - total_strips)
    offs[0] = 0
    for k in range(ns):
        target = lax.rem(me + k, ns)
        pick = 0
        for j in range(BLOCKS_DEV):
            pick = jnp.where(owner[0, me * BLOCKS_DEV + j] == target, j, pick)
        chosen[k] = pick

    hear_hello(everyone)
    place_copies = [
        remote(
            place.at[:, pl.ds(row_dev, row_reach)],
            place.at[:, pl.ds(0, row_reach)],
            sem_s.at[6, 0], sem_r.at[6, 0], "sixteen", ns, 1,
        ),
        remote(
            place.at[:, pl.ds(row_reach, row_reach)],
            place.at[:, pl.ds(row_reach + row_dev, row_reach)],
            sem_s.at[6, 1], sem_r.at[6, 1], "sixteen", ns, ns - 1,
        ),
    ]

    def halo_copies(source, target, size, send, recv, t):
        return [
            remote(
                source.at[pl.ds(rows - reach + t * size, size)],
                target.at[pl.ds(t * size, size)],
                send.at[0, t], recv.at[0, t], "sixteen", ns, 1,
            ),
            remote(
                source.at[pl.ds(t * size, size)],
                target.at[pl.ds(reach + t * size, size)],
                send.at[1, t], recv.at[1, t], "sixteen", ns, ns - 1,
            ),
        ]

    obs_copies = [halo_copies(obs, edge, 1, obs_s, obs_r, t) for t in range(reach)]
    row_copies = edge_copies(row_eff, row_edge, reach, ns, sem_s.at[8], sem_r.at[8])
    start(place_copies)

    def stage(staged, source):
        def one(k, carry):
            for pair in range(pairs):
                staged[k, pair] = source[chosen[k] * pairs + pair]
            return carry

        lax.fori_loop(0, ns, one, 0)

    start(sum(obs_copies[:early], []))
    lax.fori_loop(early, rows - reach, pack, 0)
    lax.fori_loop(rows - reach + early, rows, pack, 0)
    stage(staged_p, obs)
    p_copies = exchange_copies(staged_p, recv_p, ns, exch_s.at[0], exch_r.at[0])

    near_first = p_copies[2::2]
    bulk = [
        p_copies[:1] + near_first[0::3],
        sum(obs_copies[3:4], []),
        sum(obs_copies[4:5], []),
        sum(obs_copies[6:7], []),
        sum(obs_copies[7:8], [])+near_first[2::3]+p_copies[1::2],
        sum(obs_copies[5:6], [])+near_first[1::3],
    ]
    start(bulk[0])
    seen_t = turned(seen, lanes)
    for r in range(rows):
        weight[r] = beside(across(seen_t, 2 * r, full), across(seen_t, 2 * r + 1, full))
    one_scale = scale_in[...]
    scale[...] = jnp.concatenate([one_scale, one_scale], axis=1)
    inv = 1.0 / scale[...]
    row_eff[...] = jnp.zeros_like(row_eff)
    col_eff[...] = jnp.zeros_like(col_eff)

    spread = 2.0 * strip_rows
    cutoff = 6.0 * strip_rows
    ratio = ROOT_THREE * cutoff / spread
    unit = (4.0 * ratio * SILL_TERM) ** (1.0 / 6.0)

    def centred(first, count):
        at = pl.ds(first, count)
        coords[0, at] = (place[0, at] - (me * row_dev + row_dev // 2).astype(F32)) * (unit / cutoff)
        coords[1, at] = (place[1, at] - (group_me * cols + cols // 2).astype(F32)) * (unit / cutoff)

    def lines(target, first, blocks):
        for c in range(2):
            for pair in range(pairs):
                a = [
                    coords[c, pl.ds(first + 2 * pair + parity, blocks, stride=strip_rows), :]
                    for parity in range(2)
                ]
                for i, s in enumerate(starts):
                    x = pltpu.roll(a[0], (cols - s) % cols, 1)
                    y = pltpu.roll(a[1], (cols + span - s) % cols, 1)
                    target[i, c, :, pair * lanes : (pair + 1) * lanes] = beside(x, y)

    def prepare_own():
        centred(row_reach, row_dev)
        for c in range(2):
            t = turned(coords[c, pl.ds(row_reach, row_dev)], lanes)
            for r in range(row_dev):
                cb[c, r] = across(t, r, full)
        lines(own_oth, row_reach, BLOCKS_DEV)

    def prepare_all():
        centred(0, row_reach)
        centred(row_reach + row_dev, row_reach)
        lines(oth, 0, oth.shape[2])

    def tile_builder(source, first_block, members, together):
        def build(t, carry):
            for step in range(together):
                build_one(t * together + step)
            return carry

        def build_one(t):
            block, i = t // groups, lax.rem(t, groups)
            at = pl.multiple_of(i * GROUP, GROUP)
            first = pl.multiple_of(block * strip_rows, strip_rows)
            row_here = cb[0, pl.ds(first, strip_rows), pl.ds(at, GROUP), :].reshape(tile_rows, lanes)
            col_here = cb[1, pl.ds(first, strip_rows), pl.ds(at, GROUP), :].reshape(tile_rows, lanes)
            for n in members:
                h = block + first_block + (offs[n] if n else 0)
                row_line = source[i, 0, pl.ds(h, 1), :]
                col_line = source[i, 1, pl.ds(h, 1), :]
                for part in range(parts):
                    cut = slice(part * lanes, (part + 1) * lanes)
                    row_gap = row_line[:, cut] - row_here
                    col_gap = col_line[:, cut] - col_here
                    square = row_gap * row_gap + col_gap * col_gap
                    if n == 0:
                        distance = square * lax.rsqrt(jnp.maximum(square, 1e-30))
                    else:
                        distance = square * lax.rsqrt(square)
                    fading = jnp.maximum(unit - distance, 0.0)
                    fading = fading * fading
                    fading = fading * fading
                    decay = jnp.exp2(distance * (-ratio * LOG2E / unit))
                    lead = (distance + unit / ratio) * (distance + unit / 4.0)
                    kernel = (lead * decay) * fading
                    if n == 0:
                        kernel = kernel * (NEIGHBOURS + 1.0)
                    high = kernel.astype(jnp.bfloat16)
                    low = (kernel - high.astype(F32)).astype(jnp.bfloat16)
                    tiles[block, i, parts * n + part, 0:tile_rows] = high
                    tiles[block, i, parts * n + part, tile_rows : 2 * tile_rows] = low

        return build

    own_together = 4
    build_own = tile_builder(own_oth, 0, (0,), own_together)
    build_tile = tile_builder(oth, REACH, tuple(range(1, NEIGHBOURS + 1)), 1)

    steps = BLOCKS_DEV * groups
    shares = (0, 9, 19, 29, 42, 53, 64)

    def build_some(part):
        lax.fori_loop(shares[part] * steps // 64, shares[part + 1] * steps // 64, build_tile, 0)

    m_copies = exchange_copies(staged_m, recv_m, ns, exch_s.at[3], exch_r.at[3])
    edge_value = HUBER_EDGE
    for sweep in range(SWEEPS):
        row_buf = (row_buf0, row_buf1)[min(sweep, 1)]
        col_send = (col_send0, col_send1)[min(sweep, 1)]
        col_got = (col_got0, col_got1)[min(sweep, 1)]
        col_all = (col_all0, col_all1)[min(sweep, 1)]

        def clipped(r):
            value = (obs[r] - row_eff[pl.ds(r, 1)] - col_eff[...]) * inv
            return weight[r] * jnp.clip(value, -edge_value, edge_value)

        def row_step(r, carry):
            row_buf[0, pl.ds(r, 1)] = jnp.sum(clipped(r), axis=0, keepdims=True)
            if sweep == 0:
                row_buf[0, pl.ds(rows + r, 1)] = jnp.sum(weight[r], axis=0, keepdims=True)
            return carry

        lax.fori_loop(0, rows, row_step, 0)
        sums = spread_copies(row_buf, "wide", nw, sem_s.at[sweep], sem_r.at[sweep])
        start(sums)
        if sweep == 0:
            prepare_own()
            lax.fori_loop(0, steps // own_together, build_own, 0)
            wait(place_copies)
            prepare_all()
        build_some(3 * sweep)
        wait(sums)
        total = gathered_sum(row_buf, "wide", nw)
        if sweep == 0:
            row_cnt[...] = jnp.maximum(total[rows:], 1.0)
        row_eff[...] = row_eff[...] + scale[...] * total[:rows] / row_cnt[...]
        if sweep == SWEEPS - 1:
            start(row_copies)

            def describe(k, carry):
                for pair in range(pairs):
                    staged_m[k, pair : pair + 1] = row_eff[pl.ds(chosen[k] * pairs + pair, 1)]
                for r in range(strip_rows):
                    at = pairs + r
                    staged_m[k, at : at + 1] = place[2, pl.ds(row_reach + chosen[k] * strip_rows + r, 1)]
                return carry

            staged_m[...] = jnp.zeros_like(staged_m)
            lax.fori_loop(0, ns, describe, 0)
            start(m_copies)

        def col_step(r, carry):
            return carry + clipped(r)

        part = fold(lax.fori_loop(0, rows, col_step, jnp.zeros(full, F32)))
        col_part[0:half] = beside(part[:half], part[half:])
        count = jnp.sum(seen, axis=0, keepdims=True)
        for k in range(ns):
            owner_of = lax.rem(me + k, ns)
            col_send[k, 0:chunk] = col_part[pl.ds(pl.multiple_of(owner_of * chunk, chunk), chunk)]
            if sweep == 0:
                col_send[k, chunk : chunk + 1] = count
        sent = chunk + 1 if sweep == 0 else chunk
        col_got[0, 0:sent] = col_send[0, 0:sent]
        sums = [
            remote(
                col_send.at[k, pl.ds(0, sent)], col_got.at[k, pl.ds(0, sent)],
                sem_s.at[2 + sweep, k], sem_r.at[2 + sweep, k], "sixteen", ns, k,
            )
            for k in range(1, ns)
        ]
        start(sums)
        start(bulk[2 * sweep + 1])
        build_some(3 * sweep + 1)
        wait(sums)
        total = gathered_sum(col_got, "sixteen", ns, sent)
        col_all[0] = total[:chunk]
        if sweep == 0:
            counts = jnp.broadcast_to(total[chunk : chunk + 1], full).T
            col_cnt[...] = jnp.maximum(counts, 1.0)
        sums = spread_copies(col_all, "sixteen", ns, sem_s.at[9 + sweep], sem_r.at[9 + sweep])
        start(sums)
        start(bulk[2 * sweep + 2])
        build_some(3 * sweep + 2)
        wait(sums)
        if sweep == 0:
            start(bulk[5])
        total = jnp.concatenate(
            [col_all[lax.rem(me - o + ns, ns)] for o in range(ns)], axis=0
        )
        y = total[:half]
        z = swap(y)
        both = jnp.concatenate([beside(y, z), beside(z, y)], axis=0)
        col_eff[...] = col_eff[...] + scale[...] * both / col_cnt[...]

    for copies in obs_copies:
        wait(copies)

    def remain(r, carry):
        obs[r] = weight[r] * (obs[r] - row_eff[pl.ds(r, 1)] - col_eff[...])
        return carry

    lax.fori_loop(0, rows, remain, 0)
    p = obs

    def windows(source, first, h):
        for pair in range(pairs):
            x = source[first + pair]
            z = swap(x)
            low = low_lanes(x)
            for parity in range(2):
                y = jnp.where(low, x, z) if parity == 0 else jnp.where(low, z, x)
                high = y.astype(jnp.bfloat16).astype(F32)
                both = jnp.where(low, high, y - high)
                win[0, h, 2 * pair + parity] = both.astype(jnp.bfloat16)
                win[1, h, 2 * pair + parity, 0 : cols - GROUP] = both[
                    GROUP // 2 : cols - GROUP // 2
                ].astype(jnp.bfloat16)

    def own_windows(source):
        def one(b, carry):
            windows(source, b * pairs, REACH + b)
            return carry

        lax.fori_loop(0, BLOCKS_DEV, one, 0)

    def edge_windows(source):
        def one(b, carry):
            windows(source, b * pairs, b)
            windows(source, reach + b * pairs, REACH + BLOCKS_DEV + b)
            return carry

        lax.fori_loop(0, REACH, one, 0)

    own_windows(p)
    wait(row_copies)
    seen_t = turned(place[2], lanes)
    for t in range(reach):
        for at, r in ((t, t), (reach + t, reach + rows + t)):
            there = beside(across(seen_t, 2 * r, full), across(seen_t, 2 * r + 1, full))
            edge[at] = there * (edge[at] - row_edge[pl.ds(at, 1)] - col_eff[...])
    edge_windows(edge)
    dots[...] = jnp.zeros_like(dots)

    def apply(block, own_of, store):
        for i, s in enumerate(starts):
            shifted = (s % GROUP) // (GROUP // 2)
            base = s - shifted * (GROUP // 2)
            acc = jnp.zeros((2 * tile_rows, lanes), F32)
            for n in range(NEIGHBOURS + 1):
                h = block + REACH + offs[n]
                acc = acc + jnp.dot(
                    jnp.concatenate(
                        [tiles[block, i, parts * n + part] for part in range(parts)], axis=1
                    ),
                    win[shifted, h, :, base : base + span, :].reshape(wide, lanes),
                    preferred_element_type=F32,
                )
            y = fold(acc[:tile_rows] + acc[tile_rows:])
            for pair in range(pairs):
                even = y[(2 * pair) * GROUP : (2 * pair + 1) * GROUP]
                odd = y[(2 * pair + 1) * GROUP : (2 * pair + 2) * GROUP]
                own = own_of(pair, i * GROUP)
                store(pair, i * GROUP, own, NUGGET_TERM * own + beside(even, odd))

    def gather_dot(k, x, y):
        z = x * y
        dots[k] = dots[k] + (z[: GROUP // 2] + z[GROUP // 2 :])

    def q_copies(t):
        return halo_copies(q, q_edge, pairs, halo_s, halo_r, t)

    def first_block(block):
        def own_of(pair, at):
            return p[block * pairs + pair, at : at + GROUP, :]

        def store(pair, at, own, value):
            q[block * pairs + pair, at : at + GROUP, :] = value
            gather_dot(0, own, own)
            gather_dot(1, own, value)
            gather_dot(2, value, value)

        apply(block, own_of, store)

    def first_pass(u, carry):
        t, side = u // 2, lax.rem(u, 2)
        first_block(side * REACH + t)
        up, down = q_copies(t)

        @pl.when(side == 0)
        def _():
            down.start()

        @pl.when(side == 1)
        def _():
            up.start()

        return carry

    lax.fori_loop(0, BLOCKS_DEV, first_pass, 0)

    stage(staged_q, q)
    q_exchange = exchange_copies(staged_q, recv_q, ns, exch_s.at[1], exch_r.at[1])
    start(q_exchange[0::2])
    own_windows(q)
    wait(p_copies)
    wait(m_copies)
    facts = turned(recv_m[...].reshape(ns * 8, cols), lanes)
    for k in range(ns):
        for pair in range(pairs):
            at = 8 * k + pairs + 2 * pair
            there = beside(across(facts, at, full), across(facts, at + 1, full))
            recv_p[k, pair] = there * (recv_p[k, pair] - recv_m[k, pair : pair + 1] - col_eff[...])
    for t in range(REACH):
        wait(q_copies(t))
    start(q_exchange[1::2])
    edge_windows(q_edge)

    w_copies = exchange_copies(staged_w, recv_w, ns, exch_s.at[2], exch_r.at[2])
    one_each = ns == BLOCKS_DEV
    held = 3 if one_each else 0

    def second_block(g, carry):
        slot = lax.rem(g + 1, BLOCKS_DEV)
        block = chosen[slot] if one_each else g

        def own_of(pair, at):
            return q[block * pairs + pair, at : at + GROUP, :]

        def store(pair, at, own, value):
            gather_dot(3, own, value)
            if one_each:
                staged_w[slot, pair, at : at + GROUP, :] = value
            else:
                edge[g * pairs + pair, at : at + GROUP, :] = value

        apply(block, own_of, store)
        if one_each:
            for k in range(1, held):

                @pl.when(g == k - 1)
                def _(k=k):
                    w_copies[k].start()

        return carry

    lax.fori_loop(0, BLOCKS_DEV, second_block, 0)
    if not one_each:
        stage(staged_w, edge)

    for k in range(4):
        dot_w[0, k : k + 1] = jnp.sum(fold(dots[k]), axis=0, keepdims=True)
    dot_w[0, 4:8] = jnp.zeros((4, lanes), F32)
    sums = spread_copies(dot_w, "wide", nw, sem_s.at[4], sem_r.at[4])
    start(sums)
    wait(sums)
    dot_s[0] = gathered_sum(dot_w, "wide", nw)
    sums = spread_copies(dot_s, "sixteen", ns, sem_s.at[5], sem_r.at[5])
    start(sums)
    start((w_copies[:1] if one_each else []) + w_copies[held:])
    wait(sums)
    total = gathered_sum(dot_s, "sixteen", ns)
    m0, m1, m2, m3 = (total[k : k + 1] for k in range(4))
    alpha = m0 / m1
    norm = (m0 - 2.0 * alpha * m1) + alpha * alpha * m2
    grown = 1.0 + norm / m0
    bend = grown * (grown * m1 - 2.0 * alpha * m2) + alpha * alpha * m3
    second = norm / bend
    near = alpha + second * grown
    far = second * alpha

    turned_rows = obs_in

    def deliver(target, value_of, before=None):
        for k in range(ns if static_came else BLOCKS_DEV):
            j = lax.rem(me - k + ns, ns) if static_came else k
            slot = k if static_came else came[k]
            if before is not None:
                before(k)
            for pair in range(pairs):
                at = pl.multiple_of((j * pairs + pair) * lanes, lanes)
                turned_rows[pl.ds(at, lanes)] = value_of(slot, pair).T
        for f in range(fields):
            for r in range(strip_rows):
                line = (r // 2) * lanes + (r % 2) * fields + f
                target[f, :, r * cols : (r + 1) * cols] = turned_rows[
                    pl.ds(line, BLOCKS_DEV, stride=pairs * lanes), :
                ]

    wait(q_exchange)
    deliver(out, lambda k, pair: near * recv_p[k, pair] - far * recv_q[k, pair])
    if not static_came:
        wait(w_copies)
    deliver(
        rest,
        lambda k, pair: (recv_p[k, pair] - near * recv_q[k, pair]) + far * recv_w[k, pair],
        (lambda k: wait(w_copies[k : k + 1])) if static_came else None,
    )


def owned_table(group_map, owners, per_owner):
    total_strips = group_map.shape[0]
    member = (group_map[None, :] == jnp.arange(owners, dtype=jnp.int32)[:, None]).astype(jnp.int32)
    ranked = jnp.cumsum(member, axis=1, dtype=jnp.int32) - 1
    slot_hit = (ranked[:, :, None] == jnp.arange(per_owner, dtype=jnp.int32)[None, None, :]).astype(
        jnp.int32
    ) * member[:, :, None]
    numbers = jnp.arange(total_strips, dtype=jnp.int32)
    return jnp.sum(slot_hit * numbers[None, :, None], axis=1, dtype=jnp.int32)


def hand_over_kernel(first_in, second_in, first_out, second_out, sem):
    copies = [
        pltpu.make_async_copy(first_in, first_out, sem.at[0]),
        pltpu.make_async_copy(second_in, second_out, sem.at[1]),
    ]
    start(copies)
    wait(copies)


def on_device(observations, huber_scale, observed, jitter, owner_map, neighbours):
    fields, row_dev, col_dev = observations.shape
    nw, ns = lax.axis_size("wide"), lax.axis_size("sixteen")
    strip_rows = BLOCK // col_dev
    rows, lanes = row_dev // 2, 2 * fields
    pairs = strip_rows // 2
    reach = REACH * pairs
    shape = jax.ShapeDtypeStruct

    cut = 6 * strip_rows
    span = GROUP + 2 * cut
    starts = tuple(
        min(max(GROUP * i - cut, 0), col_dev - span) for i in range(col_dev // GROUP)
    )
    groups = len(starts)
    wide = strip_rows * span
    blocks_halo = BLOCKS_DEV + 2 * REACH

    static_came = ns == BLOCKS_DEV
    if static_came:
        came = owner_map
    else:
        my_place = lax.axis_index("sixteen")
        table = owned_table(owner_map[0], ns, BLOCKS_DEV)
        my_ids = lax.dynamic_index_in_dim(table, my_place, 0, keepdims=False)
        came = (my_place - my_ids // BLOCKS_DEV + ns) % ns

    most = max(nw, ns)
    anywhere = pl.BlockSpec(memory_space=pl.ANY)
    vm = lambda *s: pltpu.VMEM(s, F32)
    moved = (ns, pairs, col_dev, lanes)
    piece = (ns, col_dev // 2 // ns + 8, lanes)
    field = (rows, col_dev, lanes)
    place_rows = row_dev + 4 * reach
    out_shape = shape((fields, BLOCKS_DEV, BLOCK), F32)
    solution_now, residual_now = pl.pallas_call(
        functools.partial(solve_kernel, nw, ns, fields, strip_rows, starts, span, static_came),
        out_shape=((vm(*out_shape.shape) if static_came else out_shape),) * 2,
        in_specs=[anywhere if static_came else SMEM] + [anywhere] * 6,
        out_specs=(VMEM, VMEM),
        scratch_shapes=[
            pltpu.SMEM((NEIGHBOURS + 1,), jnp.int32),
            pltpu.SMEM((ns,), jnp.int32),
            pltpu.SMEM(owner_map.shape, jnp.int32),
            pltpu.SMEM((NEIGHBOURS, 1, neighbours.shape[1]), jnp.int32),
            vm(fields * row_dev, col_dev),
            vm(1, fields),
            pltpu.VMEM((row_dev, col_dev), jnp.int32),
            vm(2, row_dev, col_dev),
            vm(*field), vm(*field), vm(2 * reach, col_dev, lanes), vm(*field),
            vm(2 * reach, col_dev, lanes),
            vm(*moved), vm(*moved), vm(*moved), vm(*moved), vm(*moved), vm(*moved),
            vm(ns, 8, lanes), vm(ns, 8, lanes),
            pltpu.VMEM(
                (BLOCKS_DEV, groups, (NEIGHBOURS + 1) * wide // lanes, 2 * strip_rows * GROUP, lanes),
                jnp.bfloat16,
            ),
            pltpu.VMEM((2, blocks_halo, strip_rows, col_dev, lanes), jnp.bfloat16),
            vm(2, row_dev, col_dev, lanes),
            vm(groups, 2, blocks_halo, wide),
            vm(groups, 2, BLOCKS_DEV, wide),
            vm(3, place_rows, col_dev),
            vm(2, place_rows, col_dev),
            vm(1, lanes),
            vm(rows, lanes), vm(rows, lanes), vm(col_dev, lanes), vm(col_dev, lanes),
            vm(2 * reach, lanes),
            vm(nw, 2 * rows, lanes), vm(nw, rows, lanes),
            vm(col_dev // 2, lanes),
            vm(*piece), vm(*piece), vm(*piece), vm(*piece),
            vm(ns, col_dev // 2 // ns, lanes), vm(ns, col_dev // 2 // ns, lanes),
            vm(4, 8, lanes), vm(nw, 8, lanes), vm(ns, 8, lanes),
            pltpu.SemaphoreType.DMA((6,)),
            pltpu.SemaphoreType.DMA((11, most)), pltpu.SemaphoreType.DMA((11, most)),
            pltpu.SemaphoreType.DMA((4, ns)), pltpu.SemaphoreType.DMA((4, ns)),
            pltpu.SemaphoreType.DMA((2, reach)), pltpu.SemaphoreType.DMA((2, reach)),
            pltpu.SemaphoreType.DMA((2, REACH)), pltpu.SemaphoreType.DMA((2, REACH)),
        ],
        compiler_params=pltpu.CompilerParams(
            collective_id=0, has_side_effects=True, vmem_limit_bytes=57 * 1000 * 1000 if static_came else 66 * 1000 * 1000
        ),
    )(
        came,
        owner_map,
        jnp.transpose(neighbours, (2, 0, 1)),
        observations.reshape(fields * row_dev, col_dev),
        huber_scale.reshape(1, fields),
        observed,
        jitter,
    )
    if static_came:
        solution_now, residual_now = pl.pallas_call(
            hand_over_kernel,
            out_shape=(out_shape, out_shape),
            in_specs=[VMEM] * 2,
            out_specs=(anywhere, anywhere),
            scratch_shapes=[pltpu.SemaphoreType.DMA((2,))],
        )(
            pltpu.with_memory_space_constraint(solution_now, pltpu.VMEM),
            pltpu.with_memory_space_constraint(residual_now, pltpu.VMEM),
        )
    return solution_now[None, None], residual_now[None, None]


def solution(mesh):
    return jax.shard_map(
        on_device,
        mesh=mesh,
        in_specs=(
            P(None, "sixteen", "wide"),
            P(),
            P("sixteen", "wide"),
            P(None, "sixteen", "wide"),
            P("wide", None),
            P("wide", None, None),
        ),
        out_specs=(P("wide", "sixteen", None, None, None), P("wide", "sixteen", None, None, None)),
        check_vma=False,
    )
```

```python
import functools

import jax
import jax.numpy as jnp
from jax import lax
from jax.experimental import pallas as pl
from jax.experimental.pallas import tpu as pltpu
from jax.sharding import PartitionSpec as P

BLOCK = 512
BLOCKS_DEV = 8
REACH = 4
NEIGHBOURS = 6
SWEEPS = 2

HUBER_EDGE = 1.345
NUGGET_TERM = 1.0
SILL_TERM = 0.02
ROOT_THREE = 1.7320508075688772
LOG2E = 1.4426950408889634
GROUP = 16
MESH = pl.DeviceIdType.MESH
VMEM = pl.BlockSpec(memory_space=pltpu.VMEM)
SMEM = pl.BlockSpec(memory_space=pltpu.SMEM)
F32 = jnp.float32


def say_hello(sizes):
    barrier = pltpu.get_barrier_semaphore()
    for axis, n in sizes:
        me = lax.axis_index(axis)

        def say(k, carry, axis=axis, n=n, me=me):
            pl.semaphore_signal(
                barrier, inc=1, device_id={axis: lax.rem(me + k, n)}, device_id_type=MESH
            )
            return carry

        lax.fori_loop(1, n, say, 0)


def hear_hello(sizes):
    pl.semaphore_wait(pltpu.get_barrier_semaphore(), sum(n - 1 for _, n in sizes))


def remote(src, dst, send, recv, axis, n, shift):
    return pltpu.make_async_remote_copy(
        src_ref=src,
        dst_ref=dst,
        send_sem=send,
        recv_sem=recv,
        device_id={axis: lax.rem(lax.axis_index(axis) + shift, n)},
        device_id_type=MESH,
    )


def start(copies):
    for c in copies:
        c.start()


def wait(copies):
    for c in copies:
        c.wait()


def spread_copies(buffer, axis, n, send, recv):
    return [
        remote(buffer.at[0], buffer.at[k], send.at[k], recv.at[k], axis, n, k) for k in range(1, n)
    ]


def gathered_sum(buffer, axis, n, count=None):
    me = lax.axis_index(axis)
    total = None
    for owner in range(n):
        term = buffer[lax.rem(me - owner + n, n), 0 : buffer.shape[1] if count is None else count]
        total = term if total is None else total + term
    return total


def exchange_copies(staged, received, n, send, recv):
    return [pltpu.make_async_copy(staged.at[0], received.at[0], send.at[0])] + [
        remote(staged.at[k], received.at[k], send.at[k], recv.at[k], "sixteen", n, k)
        for k in range(1, n)
    ]


def edge_copies(source, target, reach, n, send, recv):
    rows = source.shape[0]
    return [
        remote(
            source.at[pl.ds(first, reach)],
            target.at[pl.ds(side * reach, reach)],
            send.at[side],
            recv.at[side],
            "sixteen",
            n,
            shift,
        )
        for side, first, shift in ((0, rows - reach, 1), (1, 0, n - 1))
    ]


def swap(x):
    return pltpu.roll(x, x.shape[-1] // 2, x.ndim - 1)


def fold(x):
    return x + swap(x)


def low_lanes(x):
    return lax.broadcasted_iota(jnp.int32, x.shape, x.ndim - 1) < x.shape[-1] // 2


def beside(even, odd):
    return jnp.where(low_lanes(even), even, odd)


def turned(x, size):
    rows = x.shape[0]
    if rows < size:
        x = jnp.concatenate([x, jnp.zeros((size - rows, x.shape[1]), x.dtype)], axis=0)
    return x.T


def across(x, k, shape):
    return jnp.broadcast_to(x[:, k : k + 1], shape)


def solve_kernel(
    nw, ns, fields, strip_rows, starts, span, static_came,
    came, owner_hbm, listed_hbm, obs_hbm, scale_hbm, seen_hbm, jitter_hbm,
    out, rest,
    offs, chosen, owner, listed, obs_in, scale_in, seen_in, jitter_in,
    obs, weight, edge, q, q_edge, staged_p, recv_p, staged_q, recv_q, staged_w, recv_w,
    staged_m, recv_m, tiles, win, cb, oth, own_oth, place, coords,
    scale, row_eff, row_cnt, col_eff, col_cnt, row_edge, row_buf0, row_buf1,
    col_part, col_send0, col_send1, col_got0, col_got1, col_all0, col_all1,
    dots, dot_w, dot_s,
    sem_in, sem_s, sem_r, exch_s, exch_r, obs_s, obs_r, halo_s, halo_r,
):
    rows, cols, lanes = obs.shape
    half = cols // 2
    chunk = half // ns
    pairs = strip_rows // 2
    reach = REACH * pairs
    row_dev = 2 * rows
    row_reach = 2 * reach
    groups = len(starts)
    wide = strip_rows * span
    parts = wide // lanes
    tile_rows = strip_rows * GROUP
    total_strips = BLOCKS_DEV * ns
    me = lax.axis_index("sixteen")
    group_me = lax.axis_index("wide")
    everyone = (("wide", nw), ("sixteen", ns))
    full = (cols, lanes)

    say_hello(everyone)
    arrivals = [
        pltpu.make_async_copy(source, target, sem_in.at[k])
        for k, (source, target) in enumerate(
            (
                (obs_hbm, obs_in), (scale_hbm, scale_in), (seen_hbm, seen_in),
                (jitter_hbm, jitter_in), (owner_hbm, owner), (listed_hbm, listed),
            )
        )
    ]
    start(arrivals)
    wait(arrivals)

    def pack(r, carry):
        both = jnp.concatenate(
            [obs_in[pl.ds(2 * r + parity, fields, stride=row_dev), :] for parity in range(2)],
            axis=0,
        )
        obs[r] = both.T
        return carry

    early = 3
    lax.fori_loop(0, early, pack, 0)
    lax.fori_loop(rows - reach, rows - reach + early, pack, 0)

    row_number = lax.broadcasted_iota(jnp.int32, (row_dev, cols), 0) + me * row_dev
    col_number = lax.broadcasted_iota(jnp.int32, (row_dev, cols), 1) + group_me * cols
    seen = seen_in[...].astype(F32)
    place[0, pl.ds(row_reach, row_dev)] = row_number.astype(F32) + jitter_in[0]
    place[1, pl.ds(row_reach, row_dev)] = col_number.astype(F32) + jitter_in[1]
    place[2, pl.ds(row_reach, row_dev)] = seen

    for n in range(NEIGHBOURS):
        other = listed[n, 0, 0]
        offs[n + 1] = jnp.where(other < total_strips // 2, other, other - total_strips)
    offs[0] = 0
    for k in range(ns):
        target = lax.rem(me + k, ns)
        pick = 0
        for j in range(BLOCKS_DEV):
            pick = jnp.where(owner[0, me * BLOCKS_DEV + j] == target, j, pick)
        chosen[k] = pick

    hear_hello(everyone)
    place_copies = [
        remote(
            place.at[:, pl.ds(row_dev, row_reach)],
            place.at[:, pl.ds(0, row_reach)],
            sem_s.at[6, 0], sem_r.at[6, 0], "sixteen", ns, 1,
        ),
        remote(
            place.at[:, pl.ds(row_reach, row_reach)],
            place.at[:, pl.ds(row_reach + row_dev, row_reach)],
            sem_s.at[6, 1], sem_r.at[6, 1], "sixteen", ns, ns - 1,
        ),
    ]

    def halo_copies(source, target, size, send, recv, t):
        return [
            remote(
                source.at[pl.ds(rows - reach + t * size, size)],
                target.at[pl.ds(t * size, size)],
                send.at[0, t], recv.at[0, t], "sixteen", ns, 1,
            ),
            remote(
                source.at[pl.ds(t * size, size)],
                target.at[pl.ds(reach + t * size, size)],
                send.at[1, t], recv.at[1, t], "sixteen", ns, ns - 1,
            ),
        ]

    obs_copies = [halo_copies(obs, edge, 1, obs_s, obs_r, t) for t in range(reach)]
    row_copies = edge_copies(row_eff, row_edge, reach, ns, sem_s.at[8], sem_r.at[8])
    start(place_copies)

    def stage(staged, source):
        def one(k, carry):
            for pair in range(pairs):
                staged[k, pair] = source[chosen[k] * pairs + pair]
            return carry

        lax.fori_loop(0, ns, one, 0)

    start(sum(obs_copies[:early], []))
    lax.fori_loop(early, rows - reach, pack, 0)
    lax.fori_loop(rows - reach + early, rows, pack, 0)
    stage(staged_p, obs)
    p_copies = exchange_copies(staged_p, recv_p, ns, exch_s.at[0], exch_r.at[0])

    near_first = p_copies[2::2]
    bulk = [
        p_copies[:1] + near_first[0::3],
        sum(obs_copies[3:4], []),
        sum(obs_copies[4:5], []),
        sum(obs_copies[6:7], []),
        sum(obs_copies[7:8], [])+near_first[2::3]+p_copies[1::2],
        sum(obs_copies[5:6], [])+near_first[1::3],
    ]
    start(bulk[0])
    seen_t = turned(seen, lanes)
    for r in range(rows):
        weight[r] = beside(across(seen_t, 2 * r, full), across(seen_t, 2 * r + 1, full))
    one_scale = scale_in[...]
    scale[...] = jnp.concatenate([one_scale, one_scale], axis=1)
    inv = 1.0 / scale[...]
    row_eff[...] = jnp.zeros_like(row_eff)
    col_eff[...] = jnp.zeros_like(col_eff)

    spread = 2.0 * strip_rows
    cutoff = 6.0 * strip_rows
    ratio = ROOT_THREE * cutoff / spread
    unit = (4.0 * ratio * SILL_TERM) ** (1.0 / 6.0)

    def centred(first, count):
        at = pl.ds(first, count)
        coords[0, at] = (place[0, at] - (me * row_dev + row_dev // 2).astype(F32)) * (unit / cutoff)
        coords[1, at] = (place[1, at] - (group_me * cols + cols // 2).astype(F32)) * (unit / cutoff)

    def lines(target, first, blocks):
        for c in range(2):
            for pair in range(pairs):
                a = [
                    coords[c, pl.ds(first + 2 * pair + parity, blocks, stride=strip_rows), :]
                    for parity in range(2)
                ]
                for i, s in enumerate(starts):
                    x = pltpu.roll(a[0], (cols - s) % cols, 1)
                    y = pltpu.roll(a[1], (cols + span - s) % cols, 1)
                    target[i, c, :, pair * lanes : (pair + 1) * lanes] = beside(x, y)

    def prepare_own():
        centred(row_reach, row_dev)
        for c in range(2):
            t = turned(coords[c, pl.ds(row_reach, row_dev)], lanes)
            for r in range(row_dev):
                cb[c, r] = across(t, r, full)
        lines(own_oth, row_reach, BLOCKS_DEV)

    def prepare_all():
        centred(0, row_reach)
        centred(row_reach + row_dev, row_reach)
        lines(oth, 0, oth.shape[2])

    def tile_builder(source, first_block, members, together):
        def build(t, carry):
            for step in range(together):
                build_one(t * together + step)
            return carry

        def build_one(t):
            block, i = t // groups, lax.rem(t, groups)
            at = pl.multiple_of(i * GROUP, GROUP)
            first = pl.multiple_of(block * strip_rows, strip_rows)
            row_here = cb[0, pl.ds(first, strip_rows), pl.ds(at, GROUP), :].reshape(tile_rows, lanes)
            col_here = cb[1, pl.ds(first, strip_rows), pl.ds(at, GROUP), :].reshape(tile_rows, lanes)
            for n in members:
                h = block + first_block + (offs[n] if n else 0)
                row_line = source[i, 0, pl.ds(h, 1), :]
                col_line = source[i, 1, pl.ds(h, 1), :]
                for part in range(parts):
                    cut = slice(part * lanes, (part + 1) * lanes)
                    row_gap = row_line[:, cut] - row_here
                    col_gap = col_line[:, cut] - col_here
                    square = row_gap * row_gap + col_gap * col_gap
                    if n == 0:
                        distance = square * lax.rsqrt(jnp.maximum(square, 1e-30))
                    else:
                        distance = square * lax.rsqrt(square)
                    fading = jnp.maximum(unit - distance, 0.0)
                    fading = fading * fading
                    fading = fading * fading
                    decay = jnp.exp2(distance * (-ratio * LOG2E / unit))
                    lead = (distance + unit / ratio) * (distance + unit / 4.0)
                    kernel = (lead * decay) * fading
                    if n == 0:
                        kernel = kernel * (NEIGHBOURS + 1.0)
                    high = kernel.astype(jnp.bfloat16)
                    low = (kernel - high.astype(F32)).astype(jnp.bfloat16)
                    tiles[block, i, parts * n + part, 0:tile_rows] = high
                    tiles[block, i, parts * n + part, tile_rows : 2 * tile_rows] = low

        return build

    own_together = 4
    build_own = tile_builder(own_oth, 0, (0,), own_together)
    build_tile = tile_builder(oth, REACH, tuple(range(1, NEIGHBOURS + 1)), 1)

    steps = BLOCKS_DEV * groups
    shares = (0, 8, 19, 30, 42, 53, 64)

    def build_some(part):
        lax.fori_loop(shares[part] * steps // 64, shares[part + 1] * steps // 64, build_tile, 0)

    m_copies = exchange_copies(staged_m, recv_m, ns, exch_s.at[3], exch_r.at[3])
    edge_value = HUBER_EDGE
    for sweep in range(SWEEPS):
        row_buf = (row_buf0, row_buf1)[min(sweep, 1)]
        col_send = (col_send0, col_send1)[min(sweep, 1)]
        col_got = (col_got0, col_got1)[min(sweep, 1)]
        col_all = (col_all0, col_all1)[min(sweep, 1)]

        def clipped(r):
            value = (obs[r] - row_eff[pl.ds(r, 1)] - col_eff[...]) * inv
            return weight[r] * jnp.clip(value, -edge_value, edge_value)

        def row_step(r, carry):
            row_buf[0, pl.ds(r, 1)] = jnp.sum(clipped(r), axis=0, keepdims=True)
            if sweep == 0:
                row_buf[0, pl.ds(rows + r, 1)] = jnp.sum(weight[r], axis=0, keepdims=True)
            return carry

        lax.fori_loop(0, rows, row_step, 0)
        sums = spread_copies(row_buf, "wide", nw, sem_s.at[sweep], sem_r.at[sweep])
        start(sums)
        if sweep == 0:
            prepare_own()
            lax.fori_loop(0, steps // own_together, build_own, 0)
            wait(place_copies)
            prepare_all()
        build_some(3 * sweep)
        wait(sums)
        total = gathered_sum(row_buf, "wide", nw)
        if sweep == 0:
            row_cnt[...] = jnp.maximum(total[rows:], 1.0)
        row_eff[...] = row_eff[...] + scale[...] * total[:rows] / row_cnt[...]
        if sweep == SWEEPS - 1:
            start(row_copies)

            def describe(k, carry):
                for pair in range(pairs):
                    staged_m[k, pair : pair + 1] = row_eff[pl.ds(chosen[k] * pairs + pair, 1)]
                for r in range(strip_rows):
                    at = pairs + r
                    staged_m[k, at : at + 1] = place[2, pl.ds(row_reach + chosen[k] * strip_rows + r, 1)]
                return carry

            staged_m[...] = jnp.zeros_like(staged_m)
            lax.fori_loop(0, ns, describe, 0)
            start(m_copies)

        def col_step(r, carry):
            return carry + clipped(r)

        part = fold(lax.fori_loop(0, rows, col_step, jnp.zeros(full, F32)))
        col_part[0:half] = beside(part[:half], part[half:])
        count = jnp.sum(seen, axis=0, keepdims=True)
        for k in range(ns):
            owner_of = lax.rem(me + k, ns)
            col_send[k, 0:chunk] = col_part[pl.ds(pl.multiple_of(owner_of * chunk, chunk), chunk)]
            if sweep == 0:
                col_send[k, chunk : chunk + 1] = count
        sent = chunk + 1 if sweep == 0 else chunk
        col_got[0, 0:sent] = col_send[0, 0:sent]
        sums = [
            remote(
                col_send.at[k, pl.ds(0, sent)], col_got.at[k, pl.ds(0, sent)],
                sem_s.at[2 + sweep, k], sem_r.at[2 + sweep, k], "sixteen", ns, k,
            )
            for k in range(1, ns)
        ]
        start(sums)
        start(bulk[2 * sweep + 1])
        build_some(3 * sweep + 1)
        wait(sums)
        total = gathered_sum(col_got, "sixteen", ns, sent)
        col_all[0] = total[:chunk]
        if sweep == 0:
            counts = jnp.broadcast_to(total[chunk : chunk + 1], full).T
            col_cnt[...] = jnp.maximum(counts, 1.0)
        sums = spread_copies(col_all, "sixteen", ns, sem_s.at[9 + sweep], sem_r.at[9 + sweep])
        start(sums)
        start(bulk[2 * sweep + 2])
        build_some(3 * sweep + 2)
        wait(sums)
        if sweep == 0:
            start(bulk[5])
        total = jnp.concatenate(
            [col_all[lax.rem(me - o + ns, ns)] for o in range(ns)], axis=0
        )
        y = total[:half]
        z = swap(y)
        both = jnp.concatenate([beside(y, z), beside(z, y)], axis=0)
        col_eff[...] = col_eff[...] + scale[...] * both / col_cnt[...]

    for copies in obs_copies:
        wait(copies)

    def remain(r, carry):
        obs[r] = weight[r] * (obs[r] - row_eff[pl.ds(r, 1)] - col_eff[...])
        return carry

    lax.fori_loop(0, rows, remain, 0)
    p = obs

    def windows(source, first, h):
        for pair in range(pairs):
            x = source[first + pair]
            z = swap(x)
            low = low_lanes(x)
            for parity in range(2):
                y = jnp.where(low, x, z) if parity == 0 else jnp.where(low, z, x)
                high = y.astype(jnp.bfloat16).astype(F32)
                both = jnp.where(low, high, y - high)
                win[0, h, 2 * pair + parity] = both.astype(jnp.bfloat16)
                win[1, h, 2 * pair + parity, 0 : cols - GROUP] = both[
                    GROUP // 2 : cols - GROUP // 2
                ].astype(jnp.bfloat16)

    def own_windows(source):
        def one(b, carry):
            windows(source, b * pairs, REACH + b)
            return carry

        lax.fori_loop(0, BLOCKS_DEV, one, 0)

    def edge_windows(source):
        def one(b, carry):
            windows(source, b * pairs, b)
            windows(source, reach + b * pairs, REACH + BLOCKS_DEV + b)
            return carry

        lax.fori_loop(0, REACH, one, 0)

    own_windows(p)
    wait(row_copies)
    seen_t = turned(place[2], lanes)
    for t in range(reach):
        for at, r in ((t, t), (reach + t, reach + rows + t)):
            there = beside(across(seen_t, 2 * r, full), across(seen_t, 2 * r + 1, full))
            edge[at] = there * (edge[at] - row_edge[pl.ds(at, 1)] - col_eff[...])
    edge_windows(edge)
    dots[...] = jnp.zeros_like(dots)

    def apply(block, own_of, store):
        for i, s in enumerate(starts):
            shifted = (s % GROUP) // (GROUP // 2)
            base = s - shifted * (GROUP // 2)
            acc = jnp.zeros((2 * tile_rows, lanes), F32)
            for n in range(NEIGHBOURS + 1):
                h = block + REACH + offs[n]
                acc = acc + jnp.dot(
                    jnp.concatenate(
                        [tiles[block, i, parts * n + part] for part in range(parts)], axis=1
                    ),
                    win[shifted, h, :, base : base + span, :].reshape(wide, lanes),
                    preferred_element_type=F32,
                )
            y = fold(acc[:tile_rows] + acc[tile_rows:])
            for pair in range(pairs):
                even = y[(2 * pair) * GROUP : (2 * pair + 1) * GROUP]
                odd = y[(2 * pair + 1) * GROUP : (2 * pair + 2) * GROUP]
                own = own_of(pair, i * GROUP)
                store(pair, i * GROUP, own, NUGGET_TERM * own + beside(even, odd))

    def gather_dot(k, x, y):
        z = x * y
        dots[k] = dots[k] + (z[: GROUP // 2] + z[GROUP // 2 :])

    def q_copies(t):
        return halo_copies(q, q_edge, pairs, halo_s, halo_r, t)

    def first_block(block):
        def own_of(pair, at):
            return p[block * pairs + pair, at : at + GROUP, :]

        def store(pair, at, own, value):
            q[block * pairs + pair, at : at + GROUP, :] = value
            gather_dot(0, own, own)
            gather_dot(1, own, value)
            gather_dot(2, value, value)

        apply(block, own_of, store)

    def first_pass(u, carry):
        t, side = u // 2, lax.rem(u, 2)
        first_block(side * REACH + t)
        up, down = q_copies(t)

        @pl.when(side == 0)
        def _():
            down.start()

        @pl.when(side == 1)
        def _():
            up.start()

        return carry

    lax.fori_loop(0, BLOCKS_DEV, first_pass, 0)

    stage(staged_q, q)
    q_exchange = exchange_copies(staged_q, recv_q, ns, exch_s.at[1], exch_r.at[1])
    start(q_exchange[0::2])
    own_windows(q)
    wait(p_copies)
    wait(m_copies)
    facts = turned(recv_m[...].reshape(ns * 8, cols), lanes)
    for k in range(ns):
        for pair in range(pairs):
            at = 8 * k + pairs + 2 * pair
            there = beside(across(facts, at, full), across(facts, at + 1, full))
            recv_p[k, pair] = there * (recv_p[k, pair] - recv_m[k, pair : pair + 1] - col_eff[...])
    for t in range(REACH):
        wait(q_copies(t))
    start(q_exchange[1::2])
    edge_windows(q_edge)

    w_copies = exchange_copies(staged_w, recv_w, ns, exch_s.at[2], exch_r.at[2])
    one_each = ns == BLOCKS_DEV
    held = 3 if one_each else 0

    def second_block(g, carry):
        slot = lax.rem(g + 1, BLOCKS_DEV)
        block = chosen[slot] if one_each else g

        def own_of(pair, at):
            return q[block * pairs + pair, at : at + GROUP, :]

        def store(pair, at, own, value):
            gather_dot(3, own, value)
            if one_each:
                staged_w[slot, pair, at : at + GROUP, :] = value
            else:
                edge[g * pairs + pair, at : at + GROUP, :] = value

        apply(block, own_of, store)
        if one_each:
            for k in range(1, held):

                @pl.when(g == k - 1)
                def _(k=k):
                    w_copies[k].start()

        return carry

    lax.fori_loop(0, BLOCKS_DEV, second_block, 0)
    if not one_each:
        stage(staged_w, edge)

    for k in range(4):
        dot_w[0, k : k + 1] = jnp.sum(fold(dots[k]), axis=0, keepdims=True)
    dot_w[0, 4:8] = jnp.zeros((4, lanes), F32)
    sums = spread_copies(dot_w, "wide", nw, sem_s.at[4], sem_r.at[4])
    start(sums)
    wait(sums)
    dot_s[0] = gathered_sum(dot_w, "wide", nw)
    sums = spread_copies(dot_s, "sixteen", ns, sem_s.at[5], sem_r.at[5])
    start(sums)
    start((w_copies[:1] if one_each else []) + w_copies[held:])
    wait(sums)
    total = gathered_sum(dot_s, "sixteen", ns)
    m0, m1, m2, m3 = (total[k : k + 1] for k in range(4))
    alpha = m0 / m1
    norm = (m0 - 2.0 * alpha * m1) + alpha * alpha * m2
    grown = 1.0 + norm / m0
    bend = grown * (grown * m1 - 2.0 * alpha * m2) + alpha * alpha * m3
    second = norm / bend
    near = alpha + second * grown
    far = second * alpha

    turned_rows = obs_in

    def deliver(target, value_of, before=None):
        for k in range(ns if static_came else BLOCKS_DEV):
            j = lax.rem(me - k + ns, ns) if static_came else k
            slot = k if static_came else came[k]
            if before is not None:
                before(k)
            for pair in range(pairs):
                at = pl.multiple_of((j * pairs + pair) * lanes, lanes)
                turned_rows[pl.ds(at, lanes)] = value_of(slot, pair).T
        for f in range(fields):
            for r in range(strip_rows):
                line = (r // 2) * lanes + (r % 2) * fields + f
                target[f, :, r * cols : (r + 1) * cols] = turned_rows[
                    pl.ds(line, BLOCKS_DEV, stride=pairs * lanes), :
                ]

    wait(q_exchange)
    deliver(out, lambda k, pair: near * recv_p[k, pair] - far * recv_q[k, pair])
    if not static_came:
        wait(w_copies)
    deliver(
        rest,
        lambda k, pair: (recv_p[k, pair] - near * recv_q[k, pair]) + far * recv_w[k, pair],
        (lambda k: wait(w_copies[k : k + 1])) if static_came else None,
    )


def owned_table(group_map, owners, per_owner):
    total_strips = group_map.shape[0]
    member = (group_map[None, :] == jnp.arange(owners, dtype=jnp.int32)[:, None]).astype(jnp.int32)
    ranked = jnp.cumsum(member, axis=1, dtype=jnp.int32) - 1
    slot_hit = (ranked[:, :, None] == jnp.arange(per_owner, dtype=jnp.int32)[None, None, :]).astype(
        jnp.int32
    ) * member[:, :, None]
    numbers = jnp.arange(total_strips, dtype=jnp.int32)
    return jnp.sum(slot_hit * numbers[None, :, None], axis=1, dtype=jnp.int32)


def hand_over_kernel(first_in, second_in, first_out, second_out, sem):
    copies = [
        pltpu.make_async_copy(first_in, first_out, sem.at[0]),
        pltpu.make_async_copy(second_in, second_out, sem.at[1]),
    ]
    start(copies)
    wait(copies)


def on_device(observations, huber_scale, observed, jitter, owner_map, neighbours):
    fields, row_dev, col_dev = observations.shape
    nw, ns = lax.axis_size("wide"), lax.axis_size("sixteen")
    strip_rows = BLOCK // col_dev
    rows, lanes = row_dev // 2, 2 * fields
    pairs = strip_rows // 2
    reach = REACH * pairs
    shape = jax.ShapeDtypeStruct

    cut = 6 * strip_rows
    span = GROUP + 2 * cut
    starts = tuple(
        min(max(GROUP * i - cut, 0), col_dev - span) for i in range(col_dev // GROUP)
    )
    groups = len(starts)
    wide = strip_rows * span
    blocks_halo = BLOCKS_DEV + 2 * REACH

    static_came = ns == BLOCKS_DEV
    if static_came:
        came = owner_map
    else:
        my_place = lax.axis_index("sixteen")
        table = owned_table(owner_map[0], ns, BLOCKS_DEV)
        my_ids = lax.dynamic_index_in_dim(table, my_place, 0, keepdims=False)
        came = (my_place - my_ids // BLOCKS_DEV + ns) % ns

    most = max(nw, ns)
    anywhere = pl.BlockSpec(memory_space=pl.ANY)
    vm = lambda *s: pltpu.VMEM(s, F32)
    moved = (ns, pairs, col_dev, lanes)
    piece = (ns, col_dev // 2 // ns + 8, lanes)
    field = (rows, col_dev, lanes)
    place_rows = row_dev + 4 * reach
    out_shape = shape((fields, BLOCKS_DEV, BLOCK), F32)
    solution_now, residual_now = pl.pallas_call(
        functools.partial(solve_kernel, nw, ns, fields, strip_rows, starts, span, static_came),
        out_shape=((vm(*out_shape.shape) if static_came else out_shape),) * 2,
        in_specs=[anywhere if static_came else SMEM] + [anywhere] * 6,
        out_specs=(VMEM, VMEM),
        scratch_shapes=[
            pltpu.SMEM((NEIGHBOURS + 1,), jnp.int32),
            pltpu.SMEM((ns,), jnp.int32),
            pltpu.SMEM(owner_map.shape, jnp.int32),
            pltpu.SMEM((NEIGHBOURS, 1, neighbours.shape[1]), jnp.int32),
            vm(fields * row_dev, col_dev),
            vm(1, fields),
            pltpu.VMEM((row_dev, col_dev), jnp.int32),
            vm(2, row_dev, col_dev),
            vm(*field), vm(*field), vm(2 * reach, col_dev, lanes), vm(*field),
            vm(2 * reach, col_dev, lanes),
            vm(*moved), vm(*moved), vm(*moved), vm(*moved), vm(*moved), vm(*moved),
            vm(ns, 8, lanes), vm(ns, 8, lanes),
            pltpu.VMEM(
                (BLOCKS_DEV, groups, (NEIGHBOURS + 1) * wide // lanes, 2 * strip_rows * GROUP, lanes),
                jnp.bfloat16,
            ),
            pltpu.VMEM((2, blocks_halo, strip_rows, col_dev, lanes), jnp.bfloat16),
            vm(2, row_dev, col_dev, lanes),
            vm(groups, 2, blocks_halo, wide),
            vm(groups, 2, BLOCKS_DEV, wide),
            vm(3, place_rows, col_dev),
            vm(2, place_rows, col_dev),
            vm(1, lanes),
            vm(rows, lanes), vm(rows, lanes), vm(col_dev, lanes), vm(col_dev, lanes),
            vm(2 * reach, lanes),
            vm(nw, 2 * rows, lanes), vm(nw, rows, lanes),
            vm(col_dev // 2, lanes),
            vm(*piece), vm(*piece), vm(*piece), vm(*piece),
            vm(ns, col_dev // 2 // ns, lanes), vm(ns, col_dev // 2 // ns, lanes),
            vm(4, 8, lanes), vm(nw, 8, lanes), vm(ns, 8, lanes),
            pltpu.SemaphoreType.DMA((6,)),
            pltpu.SemaphoreType.DMA((11, most)), pltpu.SemaphoreType.DMA((11, most)),
            pltpu.SemaphoreType.DMA((4, ns)), pltpu.SemaphoreType.DMA((4, ns)),
            pltpu.SemaphoreType.DMA((2, reach)), pltpu.SemaphoreType.DMA((2, reach)),
            pltpu.SemaphoreType.DMA((2, REACH)), pltpu.SemaphoreType.DMA((2, REACH)),
        ],
        compiler_params=pltpu.CompilerParams(
            collective_id=0, has_side_effects=True, vmem_limit_bytes=57 * 1000 * 1000 if static_came else 66 * 1000 * 1000
        ),
    )(
        came,
        owner_map,
        jnp.transpose(neighbours, (2, 0, 1)),
        observations.reshape(fields * row_dev, col_dev),
        huber_scale.reshape(1, fields),
        observed,
        jitter,
    )
    if static_came:
        solution_now, residual_now = pl.pallas_call(
            hand_over_kernel,
            out_shape=(out_shape, out_shape),
            in_specs=[VMEM] * 2,
            out_specs=(anywhere, anywhere),
            scratch_shapes=[pltpu.SemaphoreType.DMA((2,))],
        )(
            pltpu.with_memory_space_constraint(solution_now, pltpu.VMEM),
            pltpu.with_memory_space_constraint(residual_now, pltpu.VMEM),
        )
    return solution_now[None, None], residual_now[None, None]


def solution(mesh):
    return jax.shard_map(
        on_device,
        mesh=mesh,
        in_specs=(
            P(None, "sixteen", "wide"),
            P(),
            P("sixteen", "wide"),
            P(None, "sixteen", "wide"),
            P("wide", None),
            P("wide", None, None),
        ),
        out_specs=(P("wide", "sixteen", None, None, None), P("wide", "sixteen", None, None, None)),
        check_vma=False,
    )
```
